256 devices in a mesh: seq: 16 (over y, x), head: 16 (over z, core).
Axes of the slice: x: 4, y: 4, z: 8, core: 2. Of those that a mesh axis runs over, the one named last changes fastest.
Arguments:
- query_rows: bfloat16 [4, 8192, 8192], P(None, 'seq', 'head'), may hold values from -6 to 6
- key_rows: bfloat16 [4, 8192, 8192], P(None, 'seq', 'head'), may hold values from -6 to 6
- value_rows: bfloat16 [4, 8192, 8192], P(None, 'seq', 'head'), may hold values from -6 to 6
- prior_state: float32 [4, 64, 128, 128], P(None, 'head'), may hold values from -512 to 512
- tree_query: bfloat16 [4, 256, 8192], P(None, 'seq', 'head'), may hold values from -6 to 6
- tree_key: bfloat16 [4, 256, 8192], P(None, 'seq', 'head'), may hold values from -6 to 6
- tree_value: bfloat16 [4, 256, 8192], P(None, 'seq', 'head'), may hold values from -12 to 12
- parents: int32 [4, 256], replicated, may hold values from 0 to 254, as said below
- out_weight: bfloat16 [8192, 8192], P('head', 'seq'), may hold values from -0.0625 to 0.0625
Outputs:
- prefill_out: bfloat16 [4, 8192, 8192], P(None, 'seq', 'head')
- verified: bfloat16 [1024, 8192], P('head', 'seq')
The draws below stay inside these ranges and needn't reach their ends.
Inputs may be any that keep to these rules, and one draw needn't show every extreme that they name: parents[r, 0] is 0; for every node n >= 1, parents[r, n] lies between n - 4 and n - 1 and is at least 0.
All inputs are finite; a program needn't handle non-finite values.
Results may differ from the reference program's by a relative error of at most 0.023.
Values may be sent and summed in bfloat16 or wider, within the bound.
No kernel may reach another device: no remote copies, remote signals or barrier semaphores. Data moves between devices by JAX's collectives and lax.ppermute only.
A program may use at most 64 MiB of HBM per device.

```python
import jax
import jax.numpy as jnp
from jax import lax

D = 8192
H = 64
DH = 128
R = 4
TOK_DEV = 512
NODES = 256
HD = 8192
WINDOW = 8192
N_SEQ = 16


def draw_parents(key, part):
    backward = jax.random.randint(jax.random.fold_in(key, 11), (R, NODES), 1, 5)
    node_ids = jnp.arange(NODES).astype(jnp.int32)
    return jnp.maximum(node_ids[None, :] - backward, 0).astype(jnp.int32)


def steps_of(rng, dims, cuts, least, largest):
    factor_of = 1.0
    for axis_at, shards_of in cuts:
        steps = jax.random.uniform(jax.random.fold_in(jax.random.fold_in(rng, 6), axis_at), (shards_of,), jnp.float32, least / len(cuts), largest / len(cuts))
        factor_of = factor_of * jnp.repeat(jnp.exp(steps), dims[axis_at] // shards_of).reshape((-1,) + (1,) * (len(dims) - 1 - axis_at))
    return factor_of


def noise(own_key, shape, spread, most, cuts=(), dtype=jnp.bfloat16):
    drawn = jax.random.normal(own_key, shape, jnp.float32) * spread
    if len(cuts) > 0:
        drawn = steps_of(own_key, shape, cuts, -0.22, 0.18) * drawn
    return jnp.clip(drawn, min=-most, max=most).astype(dtype)


def setup_inputs(seed: int = 0) -> dict:
    key_of = jax.random.split(jax.random.key(seed), 10)
    return {
        "query_rows": noise(key_of[0], (R, WINDOW, HD), 1.0, 6.0, ((1, 16), (2, 16))),
        "key_rows": noise(key_of[1], (R, WINDOW, HD), 1.0, 6.0, ((1, 16), (2, 16))),
        "value_rows": noise(key_of[2], (R, WINDOW, HD), 1.0, 6.0, ((1, 16), (2, 16))),
        "prior_state": noise(key_of[3], (R, H, DH, DH), ((TOK_DEV * N_SEQ) ** 0.5), 512.0, ((1, 16),), jnp.float32),
        "tree_query": noise(key_of[4], (R, NODES, HD), 1.0, 6.0, ((1, 16), (2, 16))),
        "tree_key": noise(key_of[5], (R, NODES, HD), 1.0, 6.0, ((1, 16), (2, 16))),
        "tree_value": noise(key_of[6], (R, NODES, HD), 2.0, 12.0, ((1, 16), (2, 16))),
        "parents": draw_parents(jax.random.fold_in(key_of[9], 71), 0),
        "out_weight": noise(key_of[8], (HD, D), HD ** -0.5, 0.0625, ((0, 16), (1, 16))),
    }


epsilon = 1e-05

def head_norm(field):
    return field * lax.rsqrt(lax.optimization_barrier(jnp.mean(field * field, axis=-1, keepdims=True)) + epsilon)

def held_bf16(field):
    return lax.optimization_barrier(field.astype(jnp.bfloat16)).astype(jnp.float32)

def reference(query_rows, key_rows, value_rows, prior_state, tree_query, tree_key, tree_value, parents, out_weight):
    block = min(512, TOK_DEV)
    window = TOK_DEV * N_SEQ
    blocks = window // block
    highest = lax.Precision.HIGHEST

    def split(field):
        return field.reshape(R, blocks, block, H, DH).transpose(1, 0, 2, 3, 4)
    causal = jnp.arange(block)[:, None] >= jnp.arange(block)[None, :]

    def advance(state, inputs):
        q_block, k_block, v_block = inputs
        q_float = q_block.astype(jnp.float32)
        k_float = k_block.astype(jnp.float32)
        v_float = v_block.astype(jnp.float32)
        context = jnp.einsum('rbhd,rhde->rbhe', q_float, held_bf16(state), precision=highest)
        scores = jnp.einsum('rbhd,rchd->rhbc', q_float, k_float, precision=highest)
        weights = held_bf16(jnp.where(causal[None, None], scores, 0.0))
        inner = jnp.einsum('rhbc,rchd->rbhd', weights, v_float, precision=highest)
        block_out = head_norm(context + inner).astype(jnp.bfloat16)
        state = state + jnp.einsum('rchd,rche->rhde', k_float, v_float, precision=highest)
        return (state, block_out)
    total, outputs = lax.scan(advance, prior_state, (split(query_rows), split(key_rows), split(value_rows)))
    prefill_out = outputs.transpose(1, 0, 2, 3, 4).reshape(R, window, H * DH)
    node_ids = jnp.arange(NODES).astype(jnp.int32)
    links = (parents[:, :, None] == node_ids[None, None, :]) & (node_ids[None, :, None] >= 1)
    itself = (node_ids[:, None] == node_ids[None, :])[None]
    reach = (links | itself).astype(jnp.bfloat16)
    for level in range((NODES - 1).bit_length()):
        square = jnp.einsum('pij,pjk->pik', reach.astype(jnp.float32), reach.astype(jnp.float32), precision=highest)
        reach = jnp.minimum(square, 1.0).astype(jnp.bfloat16)
    tree_q = tree_query.reshape(R, NODES, H, DH).astype(jnp.float32)
    tree_k = tree_key.reshape(R, NODES, H, DH).astype(jnp.float32)
    tree_v = tree_value.reshape(R, NODES, H, DH).astype(jnp.float32)
    tree_context = jnp.einsum('rkhd,rhde->rkhe', tree_q, held_bf16(total), precision=highest)
    tree_scores = jnp.einsum('rkhd,rmhd->rhkm', tree_q, tree_k, precision=highest)
    tree_weights = held_bf16(jnp.where(reach[:, None] > 0, tree_scores, 0.0))
    tree_mixed = jnp.einsum('rhkm,rmhd->rkhd', tree_weights, tree_v, precision=highest)
    node_out = head_norm(tree_context + tree_mixed).astype(jnp.bfloat16).reshape(R * NODES, H * DH)
    verified = jnp.dot(node_out, out_weight, preferred_element_type=jnp.float32).astype(jnp.bfloat16)
    return (prefill_out, verified)
```

```python
import jax
import jax.numpy as jnp
from jax import lax
from jax.experimental import pallas as pl
from jax.experimental.pallas import tpu as pltpu
from jax.sharding import Mesh
from jax.sharding import PartitionSpec as P

DH = 128
NODES = 256
SEQ = ("y", "x")
HEAD = ("zp", "zl", "c")
EPS = 1e-05
BF = jnp.bfloat16
F32 = jnp.float32


def mm(a, b, ca, cb):
    return lax.dot_general(a, b, (((ca,), (cb,)), ((), ())), preferred_element_type=F32)


def normed(raw):
    return raw * lax.rsqrt(jnp.mean(raw * raw, axis=-1, keepdims=True) + EPS)


def room(mib):
    return pltpu.CompilerParams(vmem_limit_bytes=mib << 20)


def cost(flops, nbytes):
    return pl.CostEstimate(flops=flops, bytes_accessed=nbytes, transcendentals=0)


def states_body(k_ref, v_ref, tq_ref, tk_ref, tv_ref, o_ref):
    heads = o_ref.shape[0]
    nodes = tq_ref.shape[1]
    for h in range(heads):
        cols = slice(h * DH, (h + 1) * DH)
        kv = mm(k_ref[0, :, cols], v_ref[0, :, cols], 0, 0)
        o_ref[h, 0:DH, :] = kv.astype(BF)
        for j, ref in enumerate((tq_ref, tk_ref, tv_ref)):
            o_ref[h, DH + j * nodes : DH + (j + 1) * nodes, :] = ref[0, :, cols]


def block_states(k, v, tq, tk, tv):
    requests, tokens, width = k.shape
    heads, nodes = width // DH, tq.shape[1]
    rows = DH + 3 * nodes
    big = pl.BlockSpec((1, tokens, width), lambda r: (r, 0, 0))
    small = pl.BlockSpec((1, nodes, width), lambda r: (r, 0, 0))
    return pl.pallas_call(
        states_body,
        grid=(requests,),
        in_specs=[big, big, small, small, small],
        out_specs=pl.BlockSpec((heads, rows, DH), lambda r: (r, 0, 0)),
        out_shape=jax.ShapeDtypeStruct((requests * heads, rows, DH), BF),
        cost_estimate=cost(2 * requests * tokens * width * DH, 4 * requests * tokens * width),
        compiler_params=room(16),
        name="block_states",
    )(k, v, tq, tk, tv)


def reach_body(parents_ref, o_ref):
    row = lax.broadcasted_iota(jnp.int32, (NODES, NODES), 0)
    col = lax.broadcasted_iota(jnp.int32, (NODES, NODES), 1)
    links = (parents_ref[...] == row) & (col >= 1)
    reach = jnp.where(links | (row == col), 1.0, 0.0).astype(BF)
    for level in range((NODES - 1).bit_length()):
        reach = jnp.minimum(mm(reach, reach, 1, 0), 1.0).astype(BF)
    o_ref[...] = reach.astype(F32).T


def ancestors(own_parents):
    return pl.pallas_call(
        reach_body,
        out_shape=jax.ShapeDtypeStruct((NODES, NODES), F32),
        cost_estimate=cost(16 * NODES**3, 4 * NODES * NODES),
        compiler_params=room(4),
        name="ancestors",
    )(own_parents)


def inner_body(q_ref, k_ref, v_ref, o_ref):
    tokens, width = q_ref.shape[1:]
    half = tokens // 2
    for h in range(width // DH):
        cols = slice(h * DH, (h + 1) * DH)
        for part in range(2):
            rows = slice(part * half, (part + 1) * half)
            upto = (part + 1) * half
            scores = mm(q_ref[0, rows, cols], k_ref[0, 0:upto, cols], 1, 1)
            at = part * half + lax.broadcasted_iota(jnp.int32, scores.shape, 0)
            other = lax.broadcasted_iota(jnp.int32, scores.shape, 1)
            weights = jnp.where(at >= other, scores, 0.0).astype(BF)
            o_ref[0, rows, cols] = mm(weights, v_ref[0, 0:upto, cols], 1, 0)


def inside(q, k, v):
    requests, tokens, width = q.shape
    big = pl.BlockSpec((1, tokens, width), lambda r: (r, 0, 0))
    return pl.pallas_call(
        inner_body,
        grid=(requests,),
        in_specs=[big, big, big],
        out_specs=big,
        out_shape=jax.ShapeDtypeStruct(q.shape, F32),
        cost_estimate=cost(3 * requests * tokens * tokens * width, 10 * requests * tokens * width),
        compiler_params=room(24),
        name="inside",
    )(q, k, v)


def finish_body(q_ref, inner_ref, state_ref, o_ref):
    for h in range(state_ref.shape[0]):
        cols = slice(h * DH, (h + 1) * DH)
        raw = mm(q_ref[0, :, cols], state_ref[h], 1, 0) + inner_ref[0, :, cols]
        o_ref[0, :, cols] = normed(raw).astype(BF)


def finish(q, inner, states):
    requests, tokens, width = q.shape
    heads = width // DH
    big = pl.BlockSpec((1, tokens, width), lambda r: (r, 0, 0))
    return pl.pallas_call(
        finish_body,
        grid=(requests,),
        in_specs=[big, big, pl.BlockSpec((heads, DH, DH), lambda r: (r, 2, 0))],
        out_specs=big,
        out_shape=jax.ShapeDtypeStruct(q.shape, BF),
        cost_estimate=cost(2 * requests * tokens * width * DH, 8 * requests * tokens * width),
        compiler_params=room(24),
        name="finish",
    )(q, inner, states)


def tree_body(at_ref, got_ref, prior_ref, reach_ref, *refs):
    outs, hold = refs[:-1], refs[-1]
    peers = got_ref.shape[0]
    nodes = NODES // peers
    total = prior_ref[0]
    for s in range(peers):
        total = total + got_ref[s, 0:DH, :].astype(F32)

    def part(j):
        start = DH + j * nodes
        return got_ref[:, start : start + nodes, :].reshape(NODES, DH)

    q, k, v = part(0), part(1), part(2)
    weights = jnp.where(reach_ref[...] > 0, mm(q, k, 1, 1), 0.0).astype(BF)
    raw = mm(q, total.astype(BF), 1, 0) + mm(weights, v, 1, 0)
    hold[...] = normed(raw).astype(BF).reshape(hold.shape)
    for j, out in enumerate(outs):
        out[...] = hold[at_ref[1] ^ j]


def tree(at, got, prior, reach, groups):
    rows = NODES // groups
    whole = lambda a: pl.BlockSpec(a.shape, lambda i, at: (0,) * a.ndim)
    out = jax.ShapeDtypeStruct((rows, DH), BF)
    return pl.pallas_call(
        tree_body,
        grid_spec=pltpu.PrefetchScalarGridSpec(
            num_scalar_prefetch=1,
            grid=(1,),
            in_specs=[
                whole(got),
                pl.BlockSpec((1, DH, DH), lambda i, at: (at[0], 0, 0)),
                whole(reach),
            ],
            out_specs=[whole(out)] * groups,
            scratch_shapes=[pltpu.VMEM((groups, rows, DH), BF)],
        ),
        out_shape=[out] * groups,
        cost_estimate=cost(6 * NODES * NODES * DH, got.size * 2),
        compiler_params=room(8),
        name="tree",
    )(at, got, prior, reach)


def prefix_body(at_ref, got_ref, prior_ref, o_ref):
    running = prior_ref[0]
    for s in range(got_ref.shape[0]):
        o_ref[s] = running.astype(BF)
        running = running + got_ref[s, 0:DH, :].astype(F32)


def prefixes(at, got, prior):
    peers = got.shape[0]
    return pl.pallas_call(
        prefix_body,
        grid_spec=pltpu.PrefetchScalarGridSpec(
            num_scalar_prefetch=1,
            grid=(1,),
            in_specs=[
                pl.BlockSpec(got.shape, lambda i, at: (0, 0, 0)),
                pl.BlockSpec((1, DH, DH), lambda i, at: (at[0], 0, 0)),
            ],
            out_specs=pl.BlockSpec((peers, DH, DH), lambda i, at: (0, 2, 0)),
        ),
        out_shape=jax.ShapeDtypeStruct((peers, NODES + DH, DH), BF),
        cost_estimate=cost(peers * DH * DH, peers * DH * DH * 4),
        compiler_params=room(8),
        name="prefixes",
    )(at, got, prior)


def pack_body(*refs):
    pieces, o_ref = refs[:-2], refs[-1]
    for s in range(o_ref.shape[0]):
        for j, piece in enumerate(pieces):
            o_ref[s, j * piece.shape[0] : (j + 1) * piece.shape[0], :] = piece[...]


def packed(pieces, onto):
    peers = onto.shape[0]
    return pl.pallas_call(
        pack_body,
        grid=(1,),
        in_specs=[pl.BlockSpec(p.shape, lambda i: (0, 0)) for p in pieces]
        + [pl.BlockSpec(memory_space=pl.ANY)],
        out_specs=pl.BlockSpec((peers, NODES, DH), lambda i: (0, 0, 0)),
        out_shape=jax.ShapeDtypeStruct(onto.shape, BF),
        input_output_aliases={len(pieces): 0},
        cost_estimate=cost(0, peers * NODES * DH * 2),
        compiler_params=room(8),
        name="packed",
    )(*pieces, onto)


def project_body(at_ref, rows_ref, *refs):
    groups = (len(refs) - 1) // 2
    weights, outs, hold = refs[:groups], refs[groups:-1], refs[-1]
    requests = len(outs)
    heads = rows_ref.shape[0] // requests
    nodes = outs[0].shape[0]
    total = None
    for j in range(groups):
        lhs = jnp.concatenate(
            [
                jnp.concatenate([rows_ref[r * heads + h, j * nodes : (j + 1) * nodes, :] for h in range(heads)], axis=1)
                for r in range(requests)
            ],
            axis=0,
        )
        part = mm(lhs, weights[j][...], 1, 0)
        total = part if total is None else total + part
    hold[...] = total.astype(BF).reshape(hold.shape)
    for s, out in enumerate(outs):
        out[...] = hold[(at_ref[2] + s) % requests]


def project(at, rows, weights, requests):
    groups = len(weights)
    nodes = NODES // groups
    wide = weights[0].shape[1]
    whole = lambda a: pl.BlockSpec(a.shape, lambda i, at: (0,) * a.ndim)
    out = jax.ShapeDtypeStruct((nodes, wide), BF)
    return pl.pallas_call(
        project_body,
        grid_spec=pltpu.PrefetchScalarGridSpec(
            num_scalar_prefetch=1,
            grid=(1,),
            in_specs=[pl.BlockSpec((rows.shape[0], NODES, DH), lambda i, at: (0, 0, 0))]
            + [whole(w) for w in weights],
            out_specs=[whole(out)] * requests,
            scratch_shapes=[pltpu.VMEM((requests, nodes, wide), BF)],
        ),
        out_shape=[out] * requests,
        cost_estimate=cost(2 * rows.size * wide, 2 * rows.size + 2 * groups * weights[0].size),
        compiler_params=room(16),
        name="project",
    )(at, rows, *weights)


def on_device(q, k, v, prior, tq, tk, tv, parents, weight):
    requests, tokens, width = q.shape
    heads = width // DH
    y = lax.axis_index("y")
    seq_index = lax.axis_index(SEQ)
    zp = lax.axis_index("zp")
    group = lax.axis_index("zl") * 2 + lax.axis_index("c")
    at = jnp.stack([seq_index, group, zp]).astype(jnp.int32)
    pairs = lax.axis_size("zp")

    swap = [(0, 1), (1, 0)]
    quad = ("zl", "c")
    crossed = [(g, g ^ 3) for g in range(4)]

    sent = block_states(k, v, tq, tk, tv)
    got = lax.all_to_all(sent, SEQ, 0, 0, tiled=True)

    w_z = lax.ppermute(weight, "zl", swap)
    w_c = lax.ppermute(weight, "c", swap)

    reach = ancestors(lax.dynamic_slice_in_dim(parents, y, 1, 0))
    inner = inside(q, k, v)
    got, w_c, w_z, reach, inner = lax.optimization_barrier((got, w_c, w_z, reach, inner))
    w_zc = lax.ppermute(w_z, "c", swap)

    flat_prior = prior.reshape(requests * heads, DH, DH)
    mine, for_c, for_z, for_zc = tree(at, got, flat_prior, reach, 4)
    from_c = lax.ppermute(for_c, "c", swap)
    from_z = lax.ppermute(for_z, "zl", swap)
    from_zc = lax.ppermute(for_zc, quad, crossed)
    behind = prefixes(at, got, flat_prior)
    rows = lax.all_to_all(
        packed((mine, from_c, from_z, from_zc), behind), SEQ, 0, 0, tiled=True
    )

    parts = project(at, rows, (weight, w_c, w_z, w_zc), requests)
    total = parts[0].astype(F32)
    for s in range(1, pairs):
        ring = [(i, (i + s) % pairs) for i in range(pairs)]
        total = total + lax.ppermute(parts[s], "zp", ring).astype(F32)
    verified = total.astype(BF)

    prefill_out = finish(q, inner, rows)
    return prefill_out, verified


def solution(mesh):
    torus = Mesh(mesh.devices.reshape(4, 4, 4, 2, 2), (*SEQ, *HEAD))
    return jax.shard_map(
        on_device,
        mesh=torus,
        in_specs=(
            P(None, SEQ, HEAD),
            P(None, SEQ, HEAD),
            P(None, SEQ, HEAD),
            P(None, HEAD, None, None),
            P(None, SEQ, HEAD),
            P(None, SEQ, HEAD),
            P(None, SEQ, HEAD),
            P(),
            P(HEAD, SEQ),
        ),
        out_specs=(P(None, SEQ, HEAD), P(HEAD, SEQ)),
        check_vma=False,
    )
```

```python
import jax
import jax.numpy as jnp
from jax import lax
from jax.experimental import pallas as pl
from jax.experimental.pallas import tpu as pltpu
from jax.sharding import Mesh
from jax.sharding import PartitionSpec as P

DH = 128
NODES = 256
SEQ = ("y", "x")
HEAD = ("zp", "zl", "c")
EPS = 1e-05
BF = jnp.bfloat16
F32 = jnp.float32


def mm(a, b, ca, cb):
    return lax.dot_general(a, b, (((ca,), (cb,)), ((), ())), preferred_element_type=F32)


def normed(raw):
    return raw * lax.rsqrt(jnp.mean(raw * raw, axis=-1, keepdims=True) + EPS)


def room(mib):
    return pltpu.CompilerParams(vmem_limit_bytes=mib << 20)


def far(array):
    return pltpu.with_memory_space_constraint(array, pltpu.HBM)


def cost(flops, nbytes):
    return pl.CostEstimate(flops=flops, bytes_accessed=nbytes, transcendentals=0)


def states_body(k_ref, v_ref, tq_ref, tk_ref, tv_ref, o_ref):
    heads = o_ref.shape[0]
    nodes = tq_ref.shape[1]
    for h in range(heads):
        cols = slice(h * DH, (h + 1) * DH)
        kv = mm(k_ref[0, :, cols], v_ref[0, :, cols], 0, 0)
        o_ref[h, 0:DH, :] = kv.astype(BF)
        for j, ref in enumerate((tq_ref, tk_ref, tv_ref)):
            o_ref[h, DH + j * nodes : DH + (j + 1) * nodes, :] = ref[0, :, cols]


def block_states(k, v, tq, tk, tv):
    requests, tokens, width = k.shape
    heads, nodes = width // DH, tq.shape[1]
    rows = DH + 3 * nodes
    big = pl.BlockSpec((1, tokens, width), lambda r: (r, 0, 0))
    small = pl.BlockSpec((1, nodes, width), lambda r: (r, 0, 0))
    return pl.pallas_call(
        states_body,
        grid=(requests,),
        in_specs=[big, big, small, small, small],
        out_specs=pl.BlockSpec((heads, rows, DH), lambda r: (r, 0, 0)),
        out_shape=jax.ShapeDtypeStruct((requests * heads, rows, DH), BF),
        cost_estimate=cost(2 * requests * tokens * width * DH, 4 * requests * tokens * width),
        compiler_params=room(16),
        name="block_states",
    )(far(k), far(v), far(tq), far(tk), far(tv))


def reach_body(parents_ref, o_ref):
    row = lax.broadcasted_iota(jnp.int32, (NODES, NODES), 0)
    col = lax.broadcasted_iota(jnp.int32, (NODES, NODES), 1)
    links = (parents_ref[...] == row) & (col >= 1)
    reach = jnp.where(links | (row == col), 1.0, 0.0).astype(BF)
    for level in range((NODES - 1).bit_length()):
        reach = jnp.minimum(mm(reach, reach, 1, 0), 1.0).astype(BF)
    o_ref[...] = reach.astype(F32).T


def ancestors(own_parents):
    return pl.pallas_call(
        reach_body,
        out_shape=jax.ShapeDtypeStruct((NODES, NODES), F32),
        cost_estimate=cost(16 * NODES**3, 4 * NODES * NODES),
        compiler_params=room(4),
        name="ancestors",
    )(own_parents)


def inner_body(q_ref, k_ref, v_ref, o_ref):
    tokens, width = q_ref.shape[1:]
    half = tokens // 2
    for h in range(width // DH):
        cols = slice(h * DH, (h + 1) * DH)
        for part in range(2):
            rows = slice(part * half, (part + 1) * half)
            upto = (part + 1) * half
            scores = mm(q_ref[0, rows, cols], k_ref[0, 0:upto, cols], 1, 1)
            at = part * half + lax.broadcasted_iota(jnp.int32, scores.shape, 0)
            other = lax.broadcasted_iota(jnp.int32, scores.shape, 1)
            weights = jnp.where(at >= other, scores, 0.0).astype(BF)
            o_ref[0, rows, cols] = mm(weights, v_ref[0, 0:upto, cols], 1, 0)


def inside(q, k, v):
    requests, tokens, width = q.shape
    big = pl.BlockSpec((1, tokens, width), lambda r: (r, 0, 0))
    return pl.pallas_call(
        inner_body,
        grid=(requests,),
        in_specs=[big, big, big],
        out_specs=big,
        out_shape=pltpu.HBM(q.shape, F32),
        cost_estimate=cost(3 * requests * tokens * tokens * width, 10 * requests * tokens * width),
        compiler_params=room(24),
        name="inside",
    )(far(q), far(k), far(v))


def finish_body(q_ref, inner_ref, state_ref, o_ref):
    for h in range(state_ref.shape[0]):
        cols = slice(h * DH, (h + 1) * DH)
        raw = mm(q_ref[0, :, cols], state_ref[h], 1, 0) + inner_ref[0, :, cols]
        o_ref[0, :, cols] = normed(raw).astype(BF)


def finish(q, inner, states):
    requests, tokens, width = q.shape
    heads = width // DH
    big = pl.BlockSpec((1, tokens, width), lambda r: (r, 0, 0))
    return pl.pallas_call(
        finish_body,
        grid=(requests,),
        in_specs=[big, big, pl.BlockSpec((heads, DH, DH), lambda r: (r, 2, 0))],
        out_specs=big,
        out_shape=jax.ShapeDtypeStruct(q.shape, BF),
        cost_estimate=cost(2 * requests * tokens * width * DH, 8 * requests * tokens * width),
        compiler_params=room(24),
        name="finish",
    )(far(q), far(inner), states)


def tree_body(at_ref, got_ref, prior_ref, reach_ref, *refs):
    outs, hold = refs[:-1], refs[-1]
    peers = got_ref.shape[0]
    nodes = NODES // peers
    total = prior_ref[0]
    for s in range(peers):
        total = total + got_ref[s, 0:DH, :].astype(F32)

    def part(j):
        start = DH + j * nodes
        return got_ref[:, start : start + nodes, :].reshape(NODES, DH)

    q, k, v = part(0), part(1), part(2)
    weights = jnp.where(reach_ref[...] > 0, mm(q, k, 1, 1), 0.0).astype(BF)
    raw = mm(q, total.astype(BF), 1, 0) + mm(weights, v, 1, 0)
    hold[...] = normed(raw).astype(BF).reshape(hold.shape)
    for j, out in enumerate(outs):
        out[...] = hold[at_ref[1] ^ j]


def tree(at, got, prior, reach, groups):
    rows = NODES // groups
    whole = lambda a: pl.BlockSpec(a.shape, lambda i, at: (0,) * a.ndim)
    out = jax.ShapeDtypeStruct((rows, DH), BF)
    return pl.pallas_call(
        tree_body,
        grid_spec=pltpu.PrefetchScalarGridSpec(
            num_scalar_prefetch=1,
            grid=(1,),
            in_specs=[
                whole(got),
                pl.BlockSpec((1, DH, DH), lambda i, at: (at[0], 0, 0)),
                whole(reach),
            ],
            out_specs=[whole(out)] * groups,
            scratch_shapes=[pltpu.VMEM((groups, rows, DH), BF)],
        ),
        out_shape=[out] * groups,
        cost_estimate=cost(6 * NODES * NODES * DH, got.size * 2),
        compiler_params=room(8),
        name="tree",
    )(at, got, far(prior), reach)


def prefix_body(at_ref, got_ref, prior_ref, o_ref):
    running = prior_ref[0]
    for s in range(got_ref.shape[0]):
        o_ref[s] = running.astype(BF)
        running = running + got_ref[s, 0:DH, :].astype(F32)


def prefixes(at, got, prior):
    peers = got.shape[0]
    return pl.pallas_call(
        prefix_body,
        grid_spec=pltpu.PrefetchScalarGridSpec(
            num_scalar_prefetch=1,
            grid=(1,),
            in_specs=[
                pl.BlockSpec(got.shape, lambda i, at: (0, 0, 0)),
                pl.BlockSpec((1, DH, DH), lambda i, at: (at[0], 0, 0)),
            ],
            out_specs=pl.BlockSpec((peers, DH, DH), lambda i, at: (0, 2, 0)),
        ),
        out_shape=jax.ShapeDtypeStruct((peers, NODES + DH, DH), BF),
        cost_estimate=cost(peers * DH * DH, peers * DH * DH * 4),
        compiler_params=room(8),
        name="prefixes",
    )(at, got, far(prior))


def pack_body(*refs):
    pieces, o_ref = refs[:-2], refs[-1]
    for s in range(o_ref.shape[0]):
        for j, piece in enumerate(pieces):
            o_ref[s, j * piece.shape[0] : (j + 1) * piece.shape[0], :] = piece[...]


def packed(pieces, onto):
    peers = onto.shape[0]
    return pl.pallas_call(
        pack_body,
        grid=(1,),
        in_specs=[pl.BlockSpec(p.shape, lambda i: (0, 0)) for p in pieces]
        + [pl.BlockSpec(memory_space=pl.ANY)],
        out_specs=pl.BlockSpec((peers, NODES, DH), lambda i: (0, 0, 0)),
        out_shape=jax.ShapeDtypeStruct(onto.shape, BF),
        input_output_aliases={len(pieces): 0},
        cost_estimate=cost(0, peers * NODES * DH * 2),
        compiler_params=room(8),
        name="packed",
    )(*pieces, onto)


def project_body(at_ref, rows_ref, *refs):
    groups = (len(refs) - 1) // 2
    weights, outs, hold = refs[:groups], refs[groups:-1], refs[-1]
    requests = len(outs)
    heads = rows_ref.shape[0] // requests
    nodes = outs[0].shape[0]
    total = None
    for j in range(groups):
        lhs = jnp.concatenate(
            [
                jnp.concatenate([rows_ref[r * heads + h, j * nodes : (j + 1) * nodes, :] for h in range(heads)], axis=1)
                for r in range(requests)
            ],
            axis=0,
        )
        part = mm(lhs, weights[j][...], 1, 0)
        total = part if total is None else total + part
    hold[...] = total.astype(BF).reshape(hold.shape)
    for s, out in enumerate(outs):
        out[...] = hold[(at_ref[2] + s) % requests]


def project(at, rows, weights, requests):
    groups = len(weights)
    nodes = NODES // groups
    wide = weights[0].shape[1]
    whole = lambda a: pl.BlockSpec(a.shape, lambda i, at: (0,) * a.ndim)
    out = jax.ShapeDtypeStruct((nodes, wide), BF)
    return pl.pallas_call(
        project_body,
        grid_spec=pltpu.PrefetchScalarGridSpec(
            num_scalar_prefetch=1,
            grid=(1,),
            in_specs=[pl.BlockSpec((rows.shape[0], NODES, DH), lambda i, at: (0, 0, 0))]
            + [whole(w) for w in weights],
            out_specs=[whole(out)] * requests,
            scratch_shapes=[pltpu.VMEM((requests, nodes, wide), BF)],
        ),
        out_shape=[out] * requests,
        cost_estimate=cost(2 * rows.size * wide, 2 * rows.size + 2 * groups * weights[0].size),
        compiler_params=room(16),
        name="project",
    )(at, rows, *weights)


def on_device(q, k, v, prior, tq, tk, tv, parents, weight):
    requests, tokens, width = q.shape
    heads = width // DH
    y = lax.axis_index("y")
    seq_index = lax.axis_index(SEQ)
    zp = lax.axis_index("zp")
    group = lax.axis_index("zl") * 2 + lax.axis_index("c")
    at = jnp.stack([seq_index, group, zp]).astype(jnp.int32)
    pairs = lax.axis_size("zp")

    swap = [(0, 1), (1, 0)]
    quad = ("zl", "c")
    crossed = [(g, g ^ 3) for g in range(4)]

    sent = block_states(k, v, tq, tk, tv)
    got = lax.all_to_all(sent, SEQ, 0, 0, tiled=True)

    w_z = lax.ppermute(weight, "zl", swap)
    w_c = lax.ppermute(weight, "c", swap)

    reach = ancestors(lax.dynamic_slice_in_dim(parents, y, 1, 0))
    inner = inside(q, k, v)
    got, w_c, w_z, reach, inner = lax.optimization_barrier((got, w_c, w_z, reach, inner))
    w_zc = lax.ppermute(w_z, "c", swap)

    flat_prior = prior.reshape(requests * heads, DH, DH)
    mine, for_c, for_z, for_zc = tree(at, got, flat_prior, reach, 4)
    from_c = lax.ppermute(for_c, "c", swap)
    from_z = lax.ppermute(for_z, "zl", swap)
    from_zc = lax.ppermute(for_zc, quad, crossed)
    behind = prefixes(at, got, flat_prior)
    rows = lax.all_to_all(
        packed((mine, from_c, from_z, from_zc), behind), SEQ, 0, 0, tiled=True
    )

    parts = project(at, rows, (weight, w_c, w_z, w_zc), requests)
    total = parts[0].astype(F32)
    for s in range(1, pairs):
        ring = [(i, (i + s) % pairs) for i in range(pairs)]
        total = total + lax.ppermute(parts[s], "zp", ring).astype(F32)
    verified = total.astype(BF)

    prefill_out = finish(q, inner, rows)
    return prefill_out, verified


def solution(mesh):
    torus = Mesh(mesh.devices.reshape(4, 4, 4, 2, 2), (*SEQ, *HEAD))
    return jax.shard_map(
        on_device,
        mesh=torus,
        in_specs=(
            P(None, SEQ, HEAD),
            P(None, SEQ, HEAD),
            P(None, SEQ, HEAD),
            P(None, HEAD, None, None),
            P(None, SEQ, HEAD),
            P(None, SEQ, HEAD),
            P(None, SEQ, HEAD),
            P(),
            P(HEAD, SEQ),
        ),
        out_specs=(P(None, SEQ, HEAD), P(HEAD, SEQ)),
        check_vma=False,
    )
```

```python
import jax
import jax.numpy as jnp
from jax import lax
from jax.experimental import pallas as pl
from jax.experimental.pallas import tpu as pltpu
from jax.sharding import Mesh
from jax.sharding import PartitionSpec as P

DH = 128
NODES = 256
SEQ = ("y", "x")
HEAD = ("zp", "zl", "c")
EPS = 1e-05
BF = jnp.bfloat16
F32 = jnp.float32


def mm(a, b, ca, cb):
    return lax.dot_general(a, b, (((ca,), (cb,)), ((), ())), preferred_element_type=F32)


def normed(raw):
    return raw * lax.rsqrt(jnp.mean(raw * raw, axis=-1, keepdims=True) + EPS)


def room(mib):
    return pltpu.CompilerParams(vmem_limit_bytes=mib << 20)


def far(array):
    return pltpu.with_memory_space_constraint(array, pltpu.HBM)


def cost(flops, nbytes):
    return pl.CostEstimate(flops=flops, bytes_accessed=nbytes, transcendentals=0)


def states_body(k_ref, v_ref, tq_ref, tk_ref, tv_ref, o_ref):
    heads = o_ref.shape[0]
    nodes = tq_ref.shape[1]
    for h in range(heads):
        cols = slice(h * DH, (h + 1) * DH)
        kv = mm(k_ref[0, :, cols], v_ref[0, :, cols], 0, 0)
        o_ref[h, 0:DH, :] = kv.astype(BF)
        for j, ref in enumerate((tq_ref, tk_ref, tv_ref)):
            o_ref[h, DH + j * nodes : DH + (j + 1) * nodes, :] = ref[0, :, cols]


def block_states(k, v, tq, tk, tv):
    requests, tokens, width = k.shape
    heads, nodes = width // DH, tq.shape[1]
    rows = DH + 3 * nodes
    big = pl.BlockSpec((1, tokens, width), lambda r: (r, 0, 0))
    small = pl.BlockSpec((1, nodes, width), lambda r: (r, 0, 0))
    return pl.pallas_call(
        states_body,
        grid=(requests,),
        in_specs=[big, big, small, small, small],
        out_specs=pl.BlockSpec((heads, rows, DH), lambda r: (r, 0, 0)),
        out_shape=jax.ShapeDtypeStruct((requests * heads, rows, DH), BF),
        cost_estimate=cost(2 * requests * tokens * width * DH, 4 * requests * tokens * width),
        compiler_params=room(16),
        name="block_states",
    )(far(k), far(v), far(tq), far(tk), far(tv))


def reach_body(parents_ref, o_ref):
    row = lax.broadcasted_iota(jnp.int32, (NODES, NODES), 0)
    col = lax.broadcasted_iota(jnp.int32, (NODES, NODES), 1)
    links = (parents_ref[...] == row) & (col >= 1)
    reach = jnp.where(links | (row == col), 1.0, 0.0).astype(BF)
    for level in range((NODES - 1).bit_length()):
        reach = jnp.minimum(mm(reach, reach, 1, 0), 1.0).astype(BF)
    o_ref[...] = reach.astype(F32).T


def ancestors(own_parents):
    return pl.pallas_call(
        reach_body,
        out_shape=jax.ShapeDtypeStruct((NODES, NODES), F32),
        cost_estimate=cost(16 * NODES**3, 4 * NODES * NODES),
        compiler_params=room(4),
        name="ancestors",
    )(own_parents)


def inner_body(q_ref, k_ref, v_ref, o_ref):
    tokens, width = q_ref.shape[1:]
    half = tokens // 2
    for h in range(width // DH):
        cols = slice(h * DH, (h + 1) * DH)
        for part in range(2):
            rows = slice(part * half, (part + 1) * half)
            upto = (part + 1) * half
            scores = mm(q_ref[0, rows, cols], k_ref[0, 0:upto, cols], 1, 1)
            at = part * half + lax.broadcasted_iota(jnp.int32, scores.shape, 0)
            other = lax.broadcasted_iota(jnp.int32, scores.shape, 1)
            weights = jnp.where(at >= other, scores, 0.0).astype(BF)
            o_ref[0, rows, cols] = mm(weights, v_ref[0, 0:upto, cols], 1, 0).astype(BF)


def inside(q, k, v):
    requests, tokens, width = q.shape
    big = pl.BlockSpec((1, tokens, width), lambda r: (r, 0, 0))
    return pl.pallas_call(
        inner_body,
        grid=(requests,),
        in_specs=[big, big, big],
        out_specs=big,
        out_shape=pltpu.HBM(q.shape, BF),
        cost_estimate=cost(3 * requests * tokens * tokens * width, 10 * requests * tokens * width),
        compiler_params=room(24),
        name="inside",
    )(far(q), far(k), far(v))


def finish_body(q_ref, inner_ref, state_ref, o_ref):
    for h in range(state_ref.shape[0]):
        cols = slice(h * DH, (h + 1) * DH)
        raw = mm(q_ref[0, :, cols], state_ref[h], 1, 0) + inner_ref[0, :, cols].astype(F32)
        o_ref[0, :, cols] = normed(raw).astype(BF)


def finish(q, inner, states):
    requests, tokens, width = q.shape
    heads = width // DH
    big = pl.BlockSpec((1, tokens, width), lambda r: (r, 0, 0))
    return pl.pallas_call(
        finish_body,
        grid=(requests,),
        in_specs=[big, big, pl.BlockSpec((heads, DH, DH), lambda r: (r, 2, 0))],
        out_specs=big,
        out_shape=jax.ShapeDtypeStruct(q.shape, BF),
        cost_estimate=cost(2 * requests * tokens * width * DH, 8 * requests * tokens * width),
        compiler_params=room(24),
        name="finish",
    )(far(q), far(inner), states)


def smem():
    return pl.BlockSpec(memory_space=pltpu.SMEM)


def vmem(count):
    return [pl.BlockSpec(memory_space=pltpu.VMEM)] * count


def tree_body(at_ref, got_ref, prior_ref, reach_ref, *refs):
    outs, hold = refs[:-1], refs[-1]
    peers = got_ref.shape[0]
    nodes = NODES // peers
    total = prior_ref[...]
    for s in range(peers):
        total = total + got_ref[s, 0:DH, :].astype(F32)

    def part(j):
        start = DH + j * nodes
        return got_ref[:, start : start + nodes, :].reshape(NODES, DH)

    q, k, v = part(0), part(1), part(2)
    weights = jnp.where(reach_ref[...] > 0, mm(q, k, 1, 1), 0.0).astype(BF)
    raw = mm(q, total.astype(BF), 1, 0) + mm(weights, v, 1, 0)
    hold[...] = normed(raw).astype(BF).reshape(hold.shape)
    for j, out in enumerate(outs):
        out[...] = hold[at_ref[0] ^ j]


def tree(at, got, prior, reach, groups):
    rows = NODES // groups
    return pl.pallas_call(
        tree_body,
        in_specs=[smem()] + vmem(3),
        out_specs=vmem(groups),
        scratch_shapes=[pltpu.VMEM((groups, rows, DH), BF)],
        out_shape=[jax.ShapeDtypeStruct((rows, DH), BF)] * groups,
        cost_estimate=cost(6 * NODES * NODES * DH, got.size * 2),
        compiler_params=room(4),
        name="tree",
    )(at, got, prior, reach)


def prefix_body(got_ref, prior_ref, o_ref):
    running = prior_ref[...]
    for s in range(got_ref.shape[0]):
        o_ref[s] = running.astype(BF)
        running = running + got_ref[s, 0:DH, :].astype(F32)


def prefixes(got, prior):
    peers = got.shape[0]
    return pl.pallas_call(
        prefix_body,
        grid=(1,),
        in_specs=vmem(2),
        out_specs=pl.BlockSpec((peers, DH, DH), lambda i: (0, NODES // DH, 0)),
        out_shape=pltpu.HBM((peers, NODES + DH, DH), BF),
        cost_estimate=cost(peers * DH * DH, peers * DH * DH * 4),
        compiler_params=room(4),
        name="prefixes",
    )(got, prior)


def pack_body(*refs):
    pieces, o_ref = refs[:-2], refs[-1]
    for j, piece in enumerate(pieces):
        block = piece[...]
        for s in range(o_ref.shape[0]):
            o_ref[s, j * piece.shape[0] : (j + 1) * piece.shape[0], :] = block


def packed(pieces, onto):
    peers = onto.shape[0]
    return pl.pallas_call(
        pack_body,
        grid=(1,),
        in_specs=vmem(len(pieces)) + [pl.BlockSpec(memory_space=pltpu.HBM)],
        out_specs=pl.BlockSpec((peers, NODES, DH), lambda i: (0, 0, 0)),
        out_shape=pltpu.HBM(onto.shape, BF),
        input_output_aliases={len(pieces): 0},
        cost_estimate=cost(0, peers * NODES * DH * 2),
        compiler_params=room(4),
        name="packed",
    )(*pieces, onto)


def project_body(at_ref, rows_ref, *refs):
    groups = (len(refs) - 3) // 2
    weights, outs = refs[:groups], refs[groups:-3]
    hold, slab, sems = refs[-3:]
    requests = len(outs)
    heads = rows_ref.shape[0] // requests
    nodes = outs[0].shape[0]
    copies = [
        pltpu.make_async_copy(weights[j], slab.at[j], sems.at[j]) for j in range(groups)
    ]
    for copy in copies:
        copy.start()
    total = None
    for j in range(groups):
        lhs = jnp.concatenate(
            [
                jnp.concatenate(
                    [
                        rows_ref[r * heads + h, j * nodes : (j + 1) * nodes, :]
                        for h in range(heads)
                    ],
                    axis=1,
                )
                for r in range(requests)
            ],
            axis=0,
        )
        copies[j].wait()
        part = mm(lhs, slab[j], 1, 0)
        total = part if total is None else total + part
    hold[...] = total.astype(BF).reshape(hold.shape)
    for s, out in enumerate(outs):
        out[...] = hold[(at_ref[1] + s) % requests]


def project(at, rows, weights, requests):
    groups = len(weights)
    nodes = NODES // groups
    deep, wide = weights[0].shape
    peers = rows.shape[0]
    return pl.pallas_call(
        project_body,
        in_specs=[smem()] + vmem(1) + [pl.BlockSpec(memory_space=pl.ANY)] * groups,
        out_specs=vmem(requests),
        scratch_shapes=[
            pltpu.VMEM((requests, nodes, wide), BF),
            pltpu.VMEM((groups, deep, wide), BF),
            pltpu.SemaphoreType.DMA((groups,)),
        ],
        out_shape=[jax.ShapeDtypeStruct((nodes, wide), BF)] * requests,
        cost_estimate=cost(2 * peers * NODES * DH * wide, 2 * rows.size + 2 * groups * deep * wide),
        compiler_params=room(8),
        name="project",
    )(at, rows, *weights)


def on_device(q, k, v, prior, tq, tk, tv, parents, weight):
    requests, tokens, width = q.shape
    heads = width // DH
    y = lax.axis_index("y")
    zp = lax.axis_index("zp")
    group = lax.axis_index("zl") * 2 + lax.axis_index("c")
    at = jnp.stack([group, zp]).astype(jnp.int32)
    pairs = lax.axis_size("zp")

    swap = [(0, 1), (1, 0)]
    quad = ("zl", "c")
    crossed = [(g, g ^ 3) for g in range(4)]

    sent = block_states(k, v, tq, tk, tv)
    got = lax.all_to_all(sent, SEQ, 0, 0, tiled=True)

    w_z = lax.ppermute(weight, "zl", swap)
    w_c = lax.ppermute(weight, "c", swap)
    reach = ancestors(lax.dynamic_slice_in_dim(parents, y, 1, 0))
    flat_prior = prior.reshape(requests * heads, DH, DH)
    own_prior = lax.dynamic_index_in_dim(flat_prior, lax.axis_index(SEQ), 0, keepdims=False)
    got, reach, own_prior = lax.optimization_barrier((got, reach, own_prior))

    mine, for_c, for_z, for_zc = tree(at, got, own_prior, reach, 4)
    from_c = lax.ppermute(for_c, "c", swap)
    from_z = lax.ppermute(for_z, "zl", swap)
    from_zc = lax.ppermute(for_zc, quad, crossed)
    behind = prefixes(got, own_prior)
    full = packed((mine, from_c, from_z, from_zc), behind)
    full, q, k, v, w_z = lax.optimization_barrier((full, q, k, v, w_z))
    rows = lax.all_to_all(full, SEQ, 0, 0, tiled=True)
    w_zc = lax.ppermute(w_z, "c", swap)
    inner = inside(q, k, v)
    rows, inner = lax.optimization_barrier((rows, inner))

    parts = project(at, rows, (weight, w_c, w_z, w_zc), requests)
    total = parts[0].astype(F32)
    for s in range(1, pairs):
        ring = [(i, (i + s) % pairs) for i in range(pairs)]
        total = total + lax.ppermute(parts[s], "zp", ring).astype(F32)
    verified = total.astype(BF)

    prefill_out = finish(q, inner, rows)
    return prefill_out, verified


def solution(mesh):
    torus = Mesh(mesh.devices.reshape(4, 4, 4, 2, 2), (*SEQ, *HEAD))
    return jax.shard_map(
        on_device,
        mesh=torus,
        in_specs=(
            P(None, SEQ, HEAD),
            P(None, SEQ, HEAD),
            P(None, SEQ, HEAD),
            P(None, HEAD, None, None),
            P(None, SEQ, HEAD),
            P(None, SEQ, HEAD),
            P(None, SEQ, HEAD),
            P(),
            P(HEAD, SEQ),
        ),
        out_specs=(P(None, SEQ, HEAD), P(HEAD, SEQ)),
        check_vma=False,
    )
```

```python
import jax
import jax.numpy as jnp
from jax import lax
from jax.experimental import pallas as pl
from jax.experimental.pallas import tpu as pltpu
from jax.sharding import Mesh
from jax.sharding import PartitionSpec as P

DH = 128
NODES = 256
SEQ = ("y", "x")
HEAD = ("zp", "zl", "c")
SIDE = 4
EPS = 1e-05
BF = jnp.bfloat16
F32 = jnp.float32


def mm(a, b, ca, cb):
    return lax.dot_general(a, b, (((ca,), (cb,)), ((), ())), preferred_element_type=F32)


def normed(raw):
    return raw * lax.rsqrt(jnp.mean(raw * raw, axis=-1, keepdims=True) + EPS)


def room(mib):
    return pltpu.CompilerParams(vmem_limit_bytes=mib << 20)


def far(array):
    return pltpu.with_memory_space_constraint(array, pltpu.HBM)


def cost(flops, nbytes):
    return pl.CostEstimate(flops=flops, bytes_accessed=nbytes, transcendentals=0)


def smem():
    return pl.BlockSpec(memory_space=pltpu.SMEM)


def vmem(count):
    return [pl.BlockSpec(memory_space=pltpu.VMEM)] * count


def like(shape, dtype=BF):
    return jax.ShapeDtypeStruct(shape, dtype)


def small(body, outs, scratch=(), flops=0):
    def call(at, *arrays):
        nbytes = sum(a.size * a.dtype.itemsize for a in arrays)
        return pl.pallas_call(
            body,
            in_specs=[smem()] + vmem(len(arrays)),
            out_specs=vmem(len(outs)),
            out_shape=list(outs),
            scratch_shapes=list(scratch),
            cost_estimate=cost(flops, 2 * nbytes),
            compiler_params=room(8),
        )(at, *arrays)

    return call


def states_body(k_ref, v_ref, tq_ref, tk_ref, tv_ref, o_ref):
    heads = o_ref.shape[0]
    nodes = tq_ref.shape[1]
    for h in range(heads):
        cols = slice(h * DH, (h + 1) * DH)
        kv = mm(k_ref[0, :, cols], v_ref[0, :, cols], 0, 0)
        o_ref[h, 0:DH, :] = kv.astype(BF)
        for j, ref in enumerate((tq_ref, tk_ref, tv_ref)):
            o_ref[h, DH + j * nodes : DH + (j + 1) * nodes, :] = ref[0, :, cols]


def block_states(k, v, tq, tk, tv):
    requests, tokens, width = k.shape
    heads, nodes = width // DH, tq.shape[1]
    rows = DH + 3 * nodes
    big = pl.BlockSpec((1, tokens, width), lambda r: (r, 0, 0))
    small = pl.BlockSpec((1, nodes, width), lambda r: (r, 0, 0))
    return pl.pallas_call(
        states_body,
        grid=(requests,),
        in_specs=[big, big, small, small, small],
        out_specs=pl.BlockSpec((heads, rows, DH), lambda r: (r, 0, 0)),
        out_shape=like((requests * heads, rows, DH)),
        cost_estimate=cost(2 * requests * tokens * width * DH, 4 * requests * tokens * width),
        compiler_params=room(16),
        name="block_states",
    )(far(k), far(v), far(tq), far(tk), far(tv))


def reach_body(parents_ref, o_ref):
    row = lax.broadcasted_iota(jnp.int32, (NODES, NODES), 0)
    col = lax.broadcasted_iota(jnp.int32, (NODES, NODES), 1)
    links = (parents_ref[...] == row) & (col >= 1)
    reach = jnp.where(links | (row == col), 1.0, 0.0).astype(BF)
    for _ in range((NODES - 1).bit_length()):
        reach = jnp.minimum(mm(reach, reach, 1, 0), 1.0).astype(BF)
    o_ref[...] = reach.astype(F32).T


def ancestors(own_parents):
    return pl.pallas_call(
        reach_body,
        out_shape=like((NODES, NODES), F32),
        cost_estimate=cost(16 * NODES**3, 4 * NODES * NODES),
        compiler_params=room(4),
        name="ancestors",
    )(own_parents)


def tree_body(at_ref, got_ref, prior_ref, reach_ref, *refs):
    outs, hold = refs[:-1], refs[-1]
    peers = got_ref.shape[0]
    nodes = NODES // peers
    total = prior_ref[...]
    for s in range(peers):
        total = total + got_ref[s, 0:DH, :].astype(F32)

    def part(j):
        start = DH + j * nodes
        return got_ref[:, start : start + nodes, :].reshape(NODES, DH)

    q, k, v = part(0), part(1), part(2)
    weights = jnp.where(reach_ref[...] > 0, mm(q, k, 1, 1), 0.0).astype(BF)
    raw = mm(q, total.astype(BF), 1, 0) + mm(weights, v, 1, 0)
    hold[...] = normed(raw).astype(BF).reshape(hold.shape)
    for j, out in enumerate(outs):
        out[...] = hold[at_ref[3] ^ j]


def tree(at, got, prior, reach):
    nodes = NODES // SIDE
    scratch = [pltpu.VMEM((SIDE, nodes, DH), BF)]
    call = small(tree_body, [like((nodes, DH))] * SIDE, scratch, 6 * NODES * NODES * DH)
    return call(at, got, prior, reach)


def prefix_body(at_ref, got_ref, prior_ref, *refs):
    outs, hold = refs[:-1], refs[-1]
    running = prior_ref[...]
    for y in range(SIDE):
        for x in range(SIDE):
            hold[y, x] = running.astype(BF)
            running = running + got_ref[y * SIDE + x, 0:DH, :].astype(F32)
    for s, out in enumerate(outs):
        out[...] = hold[at_ref[1] ^ s]


def prefixes(at, got, prior):
    scratch = [pltpu.VMEM((SIDE, SIDE, DH, DH), BF)]
    outs = [like((SIDE, DH, DH))] * SIDE
    return small(prefix_body, outs, scratch)(at, got, prior)


def regroup_body(at_ref, *refs):
    got, outs = refs[:SIDE], refs[SIDE:]
    for s, out in enumerate(outs):
        for t in range(SIDE):
            out[at_ref[1] ^ t] = got[t][at_ref[0] ^ s]


def regrouped(at, got):
    return small(regroup_body, [like(got[0].shape)] * SIDE)(at, *got)


def join_body(at_ref, *refs):
    o_ref = refs[-1]
    rows = refs[0].shape[0]
    for j, ref in enumerate(refs[:-1]):
        o_ref[j * rows : (j + 1) * rows, :] = ref[...]


def joined(at, pieces):
    rows = sum(p.shape[0] for p in pieces)
    return small(join_body, [like((rows, DH))])(at, *pieces)[0]


def inner_body(q_ref, k_ref, v_ref, o_ref):
    tokens, width = q_ref.shape[1:]
    half = tokens // 2
    for h in range(width // DH):
        cols = slice(h * DH, (h + 1) * DH)
        for part in range(2):
            rows = slice(part * half, (part + 1) * half)
            upto = (part + 1) * half
            scores = mm(q_ref[0, rows, cols], k_ref[0, 0:upto, cols], 1, 1)
            at = part * half + lax.broadcasted_iota(jnp.int32, scores.shape, 0)
            other = lax.broadcasted_iota(jnp.int32, scores.shape, 1)
            weights = jnp.where(at >= other, scores, 0.0).astype(BF)
            o_ref[0, rows, cols] = mm(weights, v_ref[0, 0:upto, cols], 1, 0).astype(BF)


def inside(q, k, v, first, count, onto=None):
    _, tokens, width = q.shape
    big = pl.BlockSpec((1, tokens, width), lambda r: (r + first, 0, 0))
    more = [] if onto is None else [onto]
    body = inner_body if onto is None else lambda q, k, v, _, o: inner_body(q, k, v, o)
    return pl.pallas_call(
        body,
        grid=(count,),
        in_specs=[big, big, big] + [pl.BlockSpec(memory_space=pltpu.HBM)] * len(more),
        out_specs=big,
        out_shape=pltpu.HBM(q.shape, BF),
        input_output_aliases={3: 0} if more else {},
        cost_estimate=cost(3 * count * tokens * tokens * width, 8 * count * tokens * width),
        compiler_params=room(24),
        name="inside",
    )(far(q), far(k), far(v), *more)


def finish_body(at_ref, q_ref, inner_ref, *refs):
    states, o_ref, hold = refs[:SIDE], refs[SIDE], refs[SIDE + 1]
    r = pl.program_id(0)

    @pl.when(r == 0)
    def _():
        for s in range(SIDE):
            hold[at_ref[0] ^ s] = states[s][...]

    for h in range(SIDE):
        cols = slice(h * DH, (h + 1) * DH)
        raw = mm(q_ref[0, :, cols], hold[h, r], 1, 0) + inner_ref[0, :, cols].astype(F32)
        o_ref[0, :, cols] = normed(raw).astype(BF)


def finish(at, q, inner, states):
    requests, tokens, width = q.shape
    big = pl.BlockSpec((1, tokens, width), lambda r: (r, 0, 0))
    return pl.pallas_call(
        finish_body,
        grid=(requests,),
        in_specs=[smem(), big, big] + vmem(SIDE),
        out_specs=big,
        out_shape=like(q.shape),
        scratch_shapes=[pltpu.VMEM((SIDE, requests, DH, DH), BF)],
        cost_estimate=cost(2 * requests * tokens * width * DH, 6 * requests * tokens * width),
        compiler_params=room(16),
        name="finish",
    )(at, far(q), far(inner), *states)


def project_body(at_ref, *refs):
    rows, weights, outs = refs[:SIDE], refs[SIDE : 2 * SIDE], refs[2 * SIDE : 3 * SIDE]
    hold, slab, sems = refs[-3:]
    nodes = outs[0].shape[0]
    copies = [pltpu.make_async_copy(weights[j], slab.at[j], sems.at[j]) for j in range(SIDE)]
    for copy in copies:
        copy.start()
    total = None
    for j in range(SIDE):
        parts = []
        for t in range(SIDE):
            heads = [
                rows[t][pl.ds((at_ref[0] ^ h) * NODES + j * nodes, nodes), :]
                for h in range(SIDE)
            ]
            parts.append(jnp.concatenate(heads, axis=1))
        lhs = jnp.concatenate(parts, axis=0)
        copies[j].wait()
        part = mm(lhs, slab[j], 1, 0)
        total = part if total is None else total + part
    hold[...] = total.astype(BF).reshape(hold.shape)
    for s, out in enumerate(outs):
        out[...] = hold[at_ref[1] ^ at_ref[2] ^ s]


def project(at, rows, weights):
    nodes = NODES // SIDE
    deep, wide = weights[0].shape
    return pl.pallas_call(
        project_body,
        in_specs=[smem()] + vmem(SIDE) + [pl.BlockSpec(memory_space=pl.ANY)] * SIDE,
        out_specs=vmem(SIDE),
        scratch_shapes=[
            pltpu.VMEM((SIDE, nodes, wide), BF),
            pltpu.VMEM((SIDE, deep, wide), BF),
            pltpu.SemaphoreType.DMA((SIDE,)),
        ],
        out_shape=[like((nodes, wide))] * SIDE,
        cost_estimate=cost(2 * SIDE * SIDE * NODES * DH * wide, 8 * deep * wide),
        compiler_params=room(8),
        name="project",
    )(at, *rows, *weights)


def exchanged(arrays, axis):
    pairs = [[(i, i ^ s) for i in range(SIDE)] for s in range(SIDE)]
    got = {s: lax.ppermute(arrays[s], axis, pairs[s]) for s in (2, 1, 3)}
    return [arrays[0], got[1], got[2], got[3]]


def on_device(q, k, v, prior, tq, tk, tv, parents, weight):
    requests, _, _ = q.shape
    x, y, zp = (lax.axis_index(name) for name in ("x", "y", "zp"))
    group = lax.axis_index("zl") * 2 + lax.axis_index("c")
    at = jnp.stack([x, y, zp, group]).astype(jnp.int32)

    swap = [(0, 1), (1, 0)]
    quad = ("zl", "c")
    crossed = [(g, g ^ 3) for g in range(SIDE)]

    sent = block_states(k, v, tq, tk, tv)
    got = lax.all_to_all(sent, SEQ, 0, 0, tiled=True)
    weight, _ = lax.optimization_barrier((weight, sent))
    w_z = lax.ppermute(weight, "zl", swap)
    reach = ancestors(lax.dynamic_slice_in_dim(parents, y, 1, 0))
    flat_prior = prior.reshape(-1, DH, DH)
    own_prior = lax.dynamic_index_in_dim(flat_prior, y * SIDE + x, 0, keepdims=False)
    inner = inside(q, k, v, 0, requests)
    got, reach, own_prior, inner = lax.optimization_barrier((got, reach, own_prior, inner))

    pieces = tree(at, got, own_prior, reach)
    from_c = lax.ppermute(pieces[1], "c", swap)
    from_z = lax.ppermute(pieces[2], "zl", swap)
    from_zc = lax.ppermute(pieces[3], quad, crossed)
    before = prefixes(at, got, own_prior)
    mine = joined(at, (pieces[0], from_c, from_z, from_zc))
    heads = exchanged([mine] * SIDE, "x")
    above = exchanged(before, "y")
    row_of_heads = joined(at, heads)
    weight, w_z, _ = lax.optimization_barrier((weight, w_z, mine))
    w_c = lax.ppermute(weight, "c", swap)
    w_zc = lax.ppermute(w_z, "c", swap)
    rows = exchanged([row_of_heads] * SIDE, "y")
    states = exchanged(regrouped(at, above), "x")

    parts = project(at, rows, (weight, w_c, w_z, w_zc))
    total = parts[0].astype(F32)
    for got in exchanged(parts, "zp")[1:]:
        total = total + got.astype(F32)
    verified = total.astype(BF)

    prefill_out = finish(at, q, inner, states)
    return prefill_out, verified


def solution(mesh):
    torus = Mesh(mesh.devices.reshape(4, 4, 4, 2, 2), (*SEQ, *HEAD))
    return jax.shard_map(
        on_device,
        mesh=torus,
        in_specs=(
            P(None, SEQ, HEAD),
            P(None, SEQ, HEAD),
            P(None, SEQ, HEAD),
            P(None, HEAD, None, None),
            P(None, SEQ, HEAD),
            P(None, SEQ, HEAD),
            P(None, SEQ, HEAD),
            P(),
            P(HEAD, SEQ),
        ),
        out_specs=(P(None, SEQ, HEAD), P(HEAD, SEQ)),
        check_vma=False,
    )
```

```python
import jax
import jax.numpy as jnp
from jax import lax
from jax.experimental import pallas as pl
from jax.experimental.pallas import tpu as pltpu
from jax.sharding import Mesh
from jax.sharding import PartitionSpec as P

DH = 128
NODES = 256
SEQ = ("y", "x")
HEAD = ("zp", "zl", "c")
SIDE = 4
EPS = 1e-05
BF = jnp.bfloat16
F32 = jnp.float32


def mm(a, b, ca, cb):
    return lax.dot_general(a, b, (((ca,), (cb,)), ((), ())), preferred_element_type=F32)


def normed(raw):
    return raw * lax.rsqrt(jnp.mean(raw * raw, axis=-1, keepdims=True) + EPS)


def room(mib):
    return pltpu.CompilerParams(vmem_limit_bytes=mib << 20)


def far(array):
    return pltpu.with_memory_space_constraint(array, pltpu.HBM)


def cost(flops, nbytes):
    return pl.CostEstimate(flops=flops, bytes_accessed=nbytes, transcendentals=0)


def smem():
    return pl.BlockSpec(memory_space=pltpu.SMEM)


def vmem(count):
    return [pl.BlockSpec(memory_space=pltpu.VMEM)] * count


def like(shape, dtype=BF):
    return jax.ShapeDtypeStruct(shape, dtype)


def small(body, outs, scratch=(), flops=0):
    def call(at, *arrays):
        nbytes = sum(a.size * a.dtype.itemsize for a in arrays)
        return pl.pallas_call(
            body,
            in_specs=[smem()] + vmem(len(arrays)),
            out_specs=vmem(len(outs)),
            out_shape=list(outs),
            scratch_shapes=list(scratch),
            cost_estimate=cost(flops, 2 * nbytes),
            compiler_params=room(8),
        )(at, *arrays)

    return call


def states_body(k_ref, v_ref, tq_ref, tk_ref, tv_ref, o_ref, ks, vs, ts, outs, sems, done):
    requests, tokens = k_ref.shape[:2]
    nodes, half = tq_ref.shape[1], tokens // 2
    thin = [
        pltpu.make_async_copy(ref, ts.at[j], sems.at[2, j])
        for j, ref in enumerate((tq_ref, tk_ref, tv_ref))
    ]
    steps = [(r, slice(t * half, (t + 1) * half)) for r in range(requests) for t in range(2)]
    loads = [
        [
            pltpu.make_async_copy(ref.at[r, rows], buf.at[r, rows], sems.at[m, n])
            for m, (ref, buf) in enumerate(((k_ref, ks), (v_ref, vs)))
        ]
        for n, (r, rows) in enumerate(steps)
    ]
    stores = [
        pltpu.make_async_copy(
            outs.at[r * SIDE : (r + 1) * SIDE], o_ref.at[r * SIDE : (r + 1) * SIDE], done.at[r]
        )
        for r in range(requests)
    ]
    for copy in thin + sum(loads, []):
        copy.start()
    for n, (r, rows) in enumerate(steps):
        for copy in loads[n]:
            copy.wait()
        if n == 0:
            for copy in thin:
                copy.wait()
        if n % 2 == 0:
            total = [None] * SIDE
        for pair in range(SIDE // 2):
            cols = slice(2 * pair * DH, 2 * (pair + 1) * DH)
            both = mm(ks[r, rows, cols], vs[r, rows, cols], 0, 0)
            for h in range(2):
                kv = both[h * DH : (h + 1) * DH, h * DH : (h + 1) * DH]
                at = 2 * pair + h
                total[at] = kv if n % 2 == 0 else total[at] + kv
        if n % 2 == 1:
            for h in range(SIDE):
                outs[r * SIDE + h, 0:DH, :] = total[h].astype(BF)
                for j in range(3):
                    rows_at = slice(DH + j * nodes, DH + (j + 1) * nodes)
                    outs[r * SIDE + h, rows_at, :] = ts[j, r, :, h * DH : (h + 1) * DH]
            stores[r].start()
    for copy in stores:
        copy.wait()


def block_states(k, v, tq, tk, tv):
    requests, tokens, width = k.shape
    nodes = tq.shape[1]
    rows = DH + 3 * nodes
    return pl.pallas_call(
        states_body,
        in_specs=[pl.BlockSpec(memory_space=pltpu.HBM)] * 5,
        out_specs=pl.BlockSpec(memory_space=pltpu.HBM),
        out_shape=pltpu.HBM((requests * SIDE, rows, DH), BF),
        scratch_shapes=[
            pltpu.VMEM(k.shape, BF),
            pltpu.VMEM(v.shape, BF),
            pltpu.VMEM((3, *tq.shape), BF),
            pltpu.VMEM((requests * SIDE, rows, DH), BF),
            pltpu.SemaphoreType.DMA((3, 2 * requests)),
            pltpu.SemaphoreType.DMA((requests,)),
        ],
        cost_estimate=cost(2 * requests * tokens * width * DH, 4 * requests * tokens * width),
        compiler_params=room(16),
        name="block_states",
    )(far(k), far(v), far(tq), far(tk), far(tv))


def reach_body(parents_ref, o_ref):
    row = lax.broadcasted_iota(jnp.int32, (NODES, NODES), 0)
    col = lax.broadcasted_iota(jnp.int32, (NODES, NODES), 1)
    links = (parents_ref[...] == row) & (col >= 1)
    reach = jnp.where(links | (row == col), 1.0, 0.0).astype(BF)
    for _ in range((NODES - 1).bit_length()):
        reach = jnp.minimum(mm(reach, reach, 1, 0), 1.0).astype(BF)
    o_ref[...] = reach.astype(F32).T


def ancestors(own_parents):
    return pl.pallas_call(
        reach_body,
        out_shape=like((NODES, NODES), F32),
        cost_estimate=cost(16 * NODES**3, 4 * NODES * NODES),
        compiler_params=room(4),
        name="ancestors",
    )(own_parents)


def tree_body(at_ref, got_ref, prior_ref, reach_ref, *refs):
    outs, hold = refs[:-1], refs[-1]
    peers = got_ref.shape[0]
    nodes = NODES // peers
    total = prior_ref[...]
    for s in range(peers):
        total = total + got_ref[s, 0:DH, :].astype(F32)

    def part(j):
        start = DH + j * nodes
        return got_ref[:, start : start + nodes, :].reshape(NODES, DH)

    q, k, v = part(0), part(1), part(2)
    weights = jnp.where(reach_ref[...] > 0, mm(q, k, 1, 1), 0.0).astype(BF)
    raw = mm(q, total.astype(BF), 1, 0) + mm(weights, v, 1, 0)
    hold[...] = normed(raw).astype(BF).reshape(hold.shape)
    for j, out in enumerate(outs):
        out[...] = hold[at_ref[3] ^ j]


def tree(at, got, prior, reach):
    nodes = NODES // SIDE
    scratch = [pltpu.VMEM((SIDE, nodes, DH), BF)]
    call = small(tree_body, [like((nodes, DH))] * SIDE, scratch, 6 * NODES * NODES * DH)
    return call(at, got, prior, reach)


def prefix_body(at_ref, got_ref, prior_ref, *refs):
    outs, hold = refs[:-1], refs[-1]
    running = prior_ref[...]
    for y in range(SIDE):
        for x in range(SIDE):
            hold[y, x] = running.astype(BF)
            running = running + got_ref[y * SIDE + x, 0:DH, :].astype(F32)
    for s, out in enumerate(outs):
        for y in range(SIDE):
            out[y] = hold[y, at_ref[0] ^ s]


def prefixes(at, got, prior):
    scratch = [pltpu.VMEM((SIDE, SIDE, DH, DH), BF)]
    outs = [like((SIDE, DH, DH))] * SIDE
    return small(prefix_body, outs, scratch)(at, got, prior)


def regroup_body(at_ref, *refs):
    got, outs = refs[:SIDE], refs[SIDE:]
    for s, out in enumerate(outs):
        for t in range(SIDE):
            out[at_ref[0] ^ t] = got[t][at_ref[1] ^ s]


def regrouped(at, got):
    return small(regroup_body, [like(got[0].shape)] * SIDE)(at, *got)


def join_body(at_ref, *refs):
    o_ref = refs[-1]
    rows = refs[0].shape[0]
    for j, ref in enumerate(refs[:-1]):
        o_ref[j * rows : (j + 1) * rows, :] = ref[...]


def joined(at, pieces):
    rows = sum(p.shape[0] for p in pieces)
    return small(join_body, [like((rows, DH))])(at, *pieces)[0]


def inner_body(q_ref, k_ref, v_ref, o_ref):
    tokens, width = q_ref.shape[1:]
    half = tokens // 2
    for h in range(width // DH):
        cols = slice(h * DH, (h + 1) * DH)
        for part in range(2):
            rows = slice(part * half, (part + 1) * half)
            upto = (part + 1) * half
            scores = mm(q_ref[0, rows, cols], k_ref[0, 0:upto, cols], 1, 1)
            at = part * half + lax.broadcasted_iota(jnp.int32, scores.shape, 0)
            other = lax.broadcasted_iota(jnp.int32, scores.shape, 1)
            weights = jnp.where(at >= other, scores, 0.0).astype(BF)
            o_ref[0, rows, cols] = mm(weights, v_ref[0, 0:upto, cols], 1, 0).astype(BF)


def inside(q, k, v, first, count, onto=None):
    _, tokens, width = q.shape
    big = pl.BlockSpec((1, tokens, width), lambda r: (r + first, 0, 0))
    more = [] if onto is None else [onto]
    body = inner_body if onto is None else lambda q, k, v, _, o: inner_body(q, k, v, o)
    return pl.pallas_call(
        body,
        grid=(count,),
        in_specs=[big, big, big] + [pl.BlockSpec(memory_space=pltpu.HBM)] * len(more),
        out_specs=big,
        out_shape=pltpu.HBM(q.shape, BF),
        input_output_aliases={3: 0} if more else {},
        cost_estimate=cost(3 * count * tokens * tokens * width, 8 * count * tokens * width),
        compiler_params=room(24),
        name="inside",
    )(far(q), far(k), far(v), *more)


def finish_body(at_ref, q_ref, inner_ref, *refs):
    states, (o_ref, hold, outs, sems) = refs[:SIDE], refs[SIDE:]
    requests, _, _ = q_ref.shape
    for s in range(SIDE):
        hold[at_ref[1] ^ s] = states[s][...]
    stores = [pltpu.make_async_copy(outs.at[r], o_ref.at[r], sems.at[r]) for r in range(requests)]
    for r in range(requests):
        for h in range(SIDE):
            cols = slice(h * DH, (h + 1) * DH)
            raw = mm(q_ref[r, :, cols], hold[r, h], 1, 0) + inner_ref[r, :, cols].astype(F32)
            outs[r, :, cols] = normed(raw).astype(BF)
        stores[r].start()
    for copy in stores:
        copy.wait()


def finish(at, q, inner, states):
    requests, tokens, width = q.shape
    return pl.pallas_call(
        finish_body,
        in_specs=[smem()] + vmem(2 + SIDE),
        out_specs=pl.BlockSpec(memory_space=pltpu.HBM),
        out_shape=like(q.shape),
        scratch_shapes=[
            pltpu.VMEM((SIDE, requests, DH, DH), BF),
            pltpu.VMEM(q.shape, BF),
            pltpu.SemaphoreType.DMA((requests,)),
        ],
        cost_estimate=cost(2 * requests * tokens * width * DH, 6 * requests * tokens * width),
        compiler_params=room(16),
        name="finish",
    )(at, q, inner, *states)


def project_body(at_ref, *refs):
    rows, weights, outs = refs[:SIDE], refs[SIDE : 2 * SIDE], refs[2 * SIDE : 3 * SIDE]
    hold, slab, sems = refs[-3:]
    nodes = outs[0].shape[0]
    copies = [pltpu.make_async_copy(weights[j], slab.at[j], sems.at[j]) for j in range(SIDE)]
    for copy in copies:
        copy.start()
    total = None
    for j in range(SIDE):
        parts = []
        for t in range(SIDE):
            heads = [
                rows[t][pl.ds((at_ref[0] ^ h) * NODES + j * nodes, nodes), :]
                for h in range(SIDE)
            ]
            parts.append(jnp.concatenate(heads, axis=1))
        lhs = jnp.concatenate(parts, axis=0)
        copies[j].wait()
        part = mm(lhs, slab[j], 1, 0)
        total = part if total is None else total + part
    hold[...] = total.astype(BF).reshape(hold.shape)
    for s, out in enumerate(outs):
        out[...] = hold[at_ref[1] ^ at_ref[2] ^ s]


def project(at, rows, weights):
    nodes = NODES // SIDE
    deep, wide = weights[0].shape
    return pl.pallas_call(
        project_body,
        in_specs=[smem()] + vmem(SIDE) + [pl.BlockSpec(memory_space=pl.ANY)] * SIDE,
        out_specs=vmem(SIDE),
        scratch_shapes=[
            pltpu.VMEM((SIDE, nodes, wide), BF),
            pltpu.VMEM((SIDE, deep, wide), BF),
            pltpu.SemaphoreType.DMA((SIDE,)),
        ],
        out_shape=[like((nodes, wide))] * SIDE,
        cost_estimate=cost(2 * SIDE * SIDE * NODES * DH * wide, 8 * deep * wide),
        compiler_params=room(8),
        name="project",
    )(at, *rows, *weights)


def exchanged(arrays, axis):
    got = [arrays[0]]
    for s in range(1, SIDE):
        got.append(lax.ppermute(arrays[s], axis, [(i, i ^ s) for i in range(SIDE)]))
    return got


def on_device(q, k, v, prior, tq, tk, tv, parents, weight):
    requests, _, _ = q.shape
    x, y, zp = (lax.axis_index(name) for name in ("x", "y", "zp"))
    group = lax.axis_index("zl") * 2 + lax.axis_index("c")
    at = jnp.stack([x, y, zp, group]).astype(jnp.int32)

    swap = [(0, 1), (1, 0)]
    quad = ("zl", "c")
    crossed = [(g, g ^ 3) for g in range(SIDE)]

    sent = block_states(k, v, tq, tk, tv)
    got = lax.all_to_all(sent, SEQ, 0, 0, tiled=True)
    weight, _ = lax.optimization_barrier((weight, sent))
    w_z = lax.ppermute(weight, "zl", swap)
    reach = ancestors(lax.dynamic_slice_in_dim(parents, y, 1, 0))
    flat_prior = prior.reshape(-1, DH, DH)
    own_prior = lax.dynamic_index_in_dim(flat_prior, y * SIDE + x, 0, keepdims=False)
    inner = inside(q, k, v, 0, requests)
    got, reach, own_prior, inner = lax.optimization_barrier((got, reach, own_prior, inner))

    pieces = tree(at, got, own_prior, reach)
    from_c = lax.ppermute(pieces[1], "c", swap)
    from_z = lax.ppermute(pieces[2], "zl", swap)
    from_zc = lax.ppermute(pieces[3], quad, crossed)
    before = prefixes(at, got, own_prior)
    from_c, from_z, from_zc, *before = lax.optimization_barrier(
        (from_c, from_z, from_zc, *before)
    )
    mine = joined(at, (pieces[0], from_c, from_z, from_zc))
    heads = exchanged([mine] * SIDE, "x")
    beside = exchanged(before, "x")
    row_of_heads = joined(at, heads)
    rows = exchanged([row_of_heads] * SIDE, "y")
    w_c = lax.ppermute(weight, "c", swap)
    w_zc = lax.ppermute(w_z, "c", swap)
    states = exchanged(regrouped(at, beside), "y")

    parts = project(at, rows, (weight, w_c, w_z, w_zc))
    total = parts[0].astype(F32)
    shares = exchanged(parts, "zp")
    for got in shares[1:]:
        total = total + got.astype(F32)
    verified = total.astype(BF)

    prefill_out = finish(at, q, inner, states)
    return prefill_out, verified


def solution(mesh):
    torus = Mesh(mesh.devices.reshape(4, 4, 4, 2, 2), (*SEQ, *HEAD))
    return jax.shard_map(
        on_device,
        mesh=torus,
        in_specs=(
            P(None, SEQ, HEAD),
            P(None, SEQ, HEAD),
            P(None, SEQ, HEAD),
            P(None, HEAD, None, None),
            P(None, SEQ, HEAD),
            P(None, SEQ, HEAD),
            P(None, SEQ, HEAD),
            P(),
            P(HEAD, SEQ),
        ),
        out_specs=(P(None, SEQ, HEAD), P(HEAD, SEQ)),
        check_vma=False,
    )
```

```python
import jax
import jax.numpy as jnp
from jax import lax
from jax.experimental import pallas as pl
from jax.experimental.pallas import tpu as pltpu
from jax.sharding import Mesh
from jax.sharding import PartitionSpec as P

DH = 128
NODES = 256
SEQ = ("y", "x")
HEAD = ("zp", "zl", "c")
SIDE = 4
EPS = 1e-05
BF = jnp.bfloat16
F32 = jnp.float32


def mm(a, b, ca, cb):
    return lax.dot_general(a, b, (((ca,), (cb,)), ((), ())), preferred_element_type=F32)


def normed(raw):
    return raw * lax.rsqrt(jnp.mean(raw * raw, axis=-1, keepdims=True) + EPS)


def room(mib):
    return pltpu.CompilerParams(vmem_limit_bytes=mib << 20)


def far(array):
    return pltpu.with_memory_space_constraint(array, pltpu.HBM)


def cost(flops, nbytes):
    return pl.CostEstimate(flops=flops, bytes_accessed=nbytes, transcendentals=0)


def smem():
    return pl.BlockSpec(memory_space=pltpu.SMEM)


def vmem(count):
    return [pl.BlockSpec(memory_space=pltpu.VMEM)] * count


def like(shape, dtype=BF):
    return jax.ShapeDtypeStruct(shape, dtype)


def small(body, outs, scratch=(), flops=0):
    def call(at, *arrays):
        nbytes = sum(a.size * a.dtype.itemsize for a in arrays)
        return pl.pallas_call(
            body,
            in_specs=[smem()] + vmem(len(arrays)),
            out_specs=vmem(len(outs)),
            out_shape=list(outs),
            scratch_shapes=list(scratch),
            cost_estimate=cost(flops, 2 * nbytes),
            compiler_params=room(8),
        )(at, *arrays)

    return call


def states_body(k_ref, v_ref, tq_ref, tk_ref, tv_ref, o_ref, ks, vs, ts, outs, sems, done):
    requests, tokens = k_ref.shape[:2]
    nodes, half = tq_ref.shape[1], tokens // 2
    thin = [
        pltpu.make_async_copy(ref, ts.at[j], sems.at[2, j])
        for j, ref in enumerate((tq_ref, tk_ref, tv_ref))
    ]
    steps = [(r, slice(t * half, (t + 1) * half)) for r in range(requests) for t in range(2)]
    loads = [
        [
            pltpu.make_async_copy(ref.at[r, rows], buf.at[r, rows], sems.at[m, n])
            for m, (ref, buf) in enumerate(((k_ref, ks), (v_ref, vs)))
        ]
        for n, (r, rows) in enumerate(steps)
    ]
    stores = [
        pltpu.make_async_copy(
            outs.at[r * SIDE : (r + 1) * SIDE], o_ref.at[r * SIDE : (r + 1) * SIDE], done.at[r]
        )
        for r in range(requests)
    ]
    for copy in thin + sum(loads, []):
        copy.start()
    for n, (r, rows) in enumerate(steps):
        for copy in loads[n]:
            copy.wait()
        if n == 0:
            for copy in thin:
                copy.wait()
        if n % 2 == 0:
            total = [None] * SIDE
        for pair in range(SIDE // 2):
            cols = slice(2 * pair * DH, 2 * (pair + 1) * DH)
            both = mm(ks[r, rows, cols], vs[r, rows, cols], 0, 0)
            for h in range(2):
                kv = both[h * DH : (h + 1) * DH, h * DH : (h + 1) * DH]
                at = 2 * pair + h
                total[at] = kv if n % 2 == 0 else total[at] + kv
        if n % 2 == 1:
            for h in range(SIDE):
                outs[r * SIDE + h, 0:DH, :] = total[h].astype(BF)
                for j in range(3):
                    rows_at = slice(DH + j * nodes, DH + (j + 1) * nodes)
                    outs[r * SIDE + h, rows_at, :] = ts[j, r, :, h * DH : (h + 1) * DH]
            stores[r].start()
    for copy in stores:
        copy.wait()


def block_states(k, v, tq, tk, tv):
    requests, tokens, width = k.shape
    nodes = tq.shape[1]
    rows = DH + 3 * nodes
    return pl.pallas_call(
        states_body,
        in_specs=[pl.BlockSpec(memory_space=pltpu.HBM)] * 5,
        out_specs=pl.BlockSpec(memory_space=pltpu.HBM),
        out_shape=pltpu.HBM((requests * SIDE, rows, DH), BF),
        scratch_shapes=[
            pltpu.VMEM(k.shape, BF),
            pltpu.VMEM(v.shape, BF),
            pltpu.VMEM((3, *tq.shape), BF),
            pltpu.VMEM((requests * SIDE, rows, DH), BF),
            pltpu.SemaphoreType.DMA((3, 2 * requests)),
            pltpu.SemaphoreType.DMA((requests,)),
        ],
        cost_estimate=cost(2 * requests * tokens * width * DH, 4 * requests * tokens * width),
        compiler_params=room(16),
        name="block_states",
    )(far(k), far(v), far(tq), far(tk), far(tv))


def reach_body(parents_ref, o_ref):
    row = lax.broadcasted_iota(jnp.int32, (NODES, NODES), 0)
    col = lax.broadcasted_iota(jnp.int32, (NODES, NODES), 1)
    links = (parents_ref[...] == row) & (col >= 1)
    reach = jnp.where(links | (row == col), 1.0, 0.0).astype(BF)
    for _ in range((NODES - 1).bit_length()):
        reach = jnp.minimum(mm(reach, reach, 1, 0), 1.0).astype(BF)
    o_ref[...] = reach.astype(F32).T


def ancestors(own_parents):
    return pl.pallas_call(
        reach_body,
        out_shape=like((NODES, NODES), F32),
        cost_estimate=cost(16 * NODES**3, 4 * NODES * NODES),
        compiler_params=room(4),
        name="ancestors",
    )(own_parents)


def tree_body(at_ref, got_ref, prior_ref, reach_ref, *refs):
    outs, hold = refs[:-1], refs[-1]
    peers = got_ref.shape[0]
    nodes = NODES // peers
    total = prior_ref[...]
    for s in range(peers):
        total = total + got_ref[s, 0:DH, :].astype(F32)

    def part(j):
        start = DH + j * nodes
        return got_ref[:, start : start + nodes, :].reshape(NODES, DH)

    q, k, v = part(0), part(1), part(2)
    weights = jnp.where(reach_ref[...] > 0, mm(q, k, 1, 1), 0.0).astype(BF)
    raw = mm(q, total.astype(BF), 1, 0) + mm(weights, v, 1, 0)
    hold[...] = normed(raw).astype(BF).reshape(hold.shape)
    for j, out in enumerate(outs):
        out[...] = hold[at_ref[3] ^ j]


def tree(at, got, prior, reach):
    nodes = NODES // SIDE
    scratch = [pltpu.VMEM((SIDE, nodes, DH), BF)]
    call = small(tree_body, [like((nodes, DH))] * SIDE, scratch, 6 * NODES * NODES * DH)
    return call(at, got, prior, reach)


def prefix_body(at_ref, got_ref, prior_ref, *refs):
    outs, hold = refs[:-1], refs[-1]
    running = prior_ref[...]
    for y in range(SIDE):
        for x in range(SIDE):
            hold[y, x] = running.astype(BF)
            running = running + got_ref[y * SIDE + x, 0:DH, :].astype(F32)
    for s, out in enumerate(outs):
        for y in range(SIDE):
            out[y] = hold[y, at_ref[0] ^ s]


def prefixes(at, got, prior):
    scratch = [pltpu.VMEM((SIDE, SIDE, DH, DH), BF)]
    outs = [like((SIDE, DH, DH))] * SIDE
    return small(prefix_body, outs, scratch)(at, got, prior)


def regroup_body(at_ref, *refs):
    got, outs = refs[:SIDE], refs[SIDE:]
    for s, out in enumerate(outs):
        for t in range(SIDE):
            out[at_ref[0] ^ t] = got[t][at_ref[1] ^ s]


def regrouped(at, got):
    return small(regroup_body, [like(got[0].shape)] * SIDE)(at, *got)


def inner_body(q_ref, k_ref, v_ref, o_ref):
    tokens, width = q_ref.shape[1:]
    half = tokens // 2
    for h in range(width // DH):
        cols = slice(h * DH, (h + 1) * DH)
        for part in range(2):
            rows = slice(part * half, (part + 1) * half)
            upto = (part + 1) * half
            scores = mm(q_ref[0, rows, cols], k_ref[0, 0:upto, cols], 1, 1)
            at = part * half + lax.broadcasted_iota(jnp.int32, scores.shape, 0)
            other = lax.broadcasted_iota(jnp.int32, scores.shape, 1)
            weights = jnp.where(at >= other, scores, 0.0).astype(BF)
            o_ref[0, rows, cols] = mm(weights, v_ref[0, 0:upto, cols], 1, 0).astype(BF)


def inside(q, k, v, first, count, onto=None):
    _, tokens, width = q.shape
    big = pl.BlockSpec((1, tokens, width), lambda r: (r + first, 0, 0))
    more = [] if onto is None else [onto]
    body = inner_body if onto is None else lambda q, k, v, _, o: inner_body(q, k, v, o)
    return pl.pallas_call(
        body,
        grid=(count,),
        in_specs=[big, big, big] + [pl.BlockSpec(memory_space=pltpu.HBM)] * len(more),
        out_specs=big,
        out_shape=pltpu.HBM(q.shape, BF),
        input_output_aliases={3: 0} if more else {},
        cost_estimate=cost(3 * count * tokens * tokens * width, 8 * count * tokens * width),
        compiler_params=room(24),
        name="inside",
    )(far(q), far(k), far(v), *more)


def finish_body(at_ref, q_ref, inner_ref, *refs):
    states, (o_ref, hold, outs, sems) = refs[:SIDE], refs[SIDE:]
    requests, _, _ = q_ref.shape
    for s in range(SIDE):
        hold[at_ref[1] ^ s] = states[s][...]
    stores = [pltpu.make_async_copy(outs.at[r], o_ref.at[r], sems.at[r]) for r in range(requests)]
    for r in range(requests):
        for h in range(SIDE):
            cols = slice(h * DH, (h + 1) * DH)
            raw = mm(q_ref[r, :, cols], hold[r, h], 1, 0) + inner_ref[r, :, cols].astype(F32)
            outs[r, :, cols] = normed(raw).astype(BF)
        stores[r].start()
    for copy in stores:
        copy.wait()


def finish(at, q, inner, states):
    requests, tokens, width = q.shape
    return pl.pallas_call(
        finish_body,
        in_specs=[smem()] + vmem(2 + SIDE),
        out_specs=pl.BlockSpec(memory_space=pltpu.HBM),
        out_shape=like(q.shape),
        scratch_shapes=[
            pltpu.VMEM((SIDE, requests, DH, DH), BF),
            pltpu.VMEM(q.shape, BF),
            pltpu.SemaphoreType.DMA((requests,)),
        ],
        cost_estimate=cost(2 * requests * tokens * width * DH, 6 * requests * tokens * width),
        compiler_params=room(16),
        name="finish",
    )(at, q, inner, *states)


def project_body(at_ref, *refs):
    rows, weights, outs = refs[:SIDE], refs[SIDE : 2 * SIDE], refs[2 * SIDE : 3 * SIDE]
    hold, slab, sems = refs[-3:]
    nodes = outs[0].shape[0]
    copies = [pltpu.make_async_copy(weights[j], slab.at[j], sems.at[j]) for j in range(SIDE)]
    for copy in copies:
        copy.start()
    total = None
    for j in range(SIDE):
        parts = []
        for t in range(SIDE):
            heads = [
                rows[t][pl.ds((at_ref[0] ^ h) * NODES + j * nodes, nodes), :]
                for h in range(SIDE)
            ]
            parts.append(jnp.concatenate(heads, axis=1))
        lhs = jnp.concatenate(parts, axis=0)
        copies[j].wait()
        part = mm(lhs, slab[j], 1, 0)
        total = part if total is None else total + part
    hold[...] = total.astype(BF).reshape(hold.shape)
    for s, out in enumerate(outs):
        out[...] = hold[at_ref[1] ^ at_ref[2] ^ s]


def project(at, rows, weights):
    nodes = NODES // SIDE
    deep, wide = weights[0].shape
    return pl.pallas_call(
        project_body,
        in_specs=[smem()] + vmem(SIDE) + [pl.BlockSpec(memory_space=pl.ANY)] * SIDE,
        out_specs=vmem(SIDE),
        scratch_shapes=[
            pltpu.VMEM((SIDE, nodes, wide), BF),
            pltpu.VMEM((SIDE, deep, wide), BF),
            pltpu.SemaphoreType.DMA((SIDE,)),
        ],
        out_shape=[like((nodes, wide))] * SIDE,
        cost_estimate=cost(2 * SIDE * SIDE * NODES * DH * wide, 8 * deep * wide),
        compiler_params=room(8),
        name="project",
    )(at, *rows, *weights)


def exchanged(arrays, axis):
    got = [arrays[0]]
    for s in range(1, SIDE):
        got.append(lax.ppermute(arrays[s], axis, [(i, i ^ s) for i in range(SIDE)]))
    return got


def on_device(q, k, v, prior, tq, tk, tv, parents, weight):
    requests, _, _ = q.shape
    x, y, zp = (lax.axis_index(name) for name in ("x", "y", "zp"))
    group = lax.axis_index("zl") * 2 + lax.axis_index("c")
    at = jnp.stack([x, y, zp, group]).astype(jnp.int32)

    swap = [(0, 1), (1, 0)]
    quad = ("zl", "c")
    crossed = [(g, g ^ 3) for g in range(SIDE)]

    sent = block_states(k, v, tq, tk, tv)
    got = lax.all_to_all(sent, SEQ, 0, 0, tiled=True)
    weight, _ = lax.optimization_barrier((weight, sent))
    w_z = lax.ppermute(weight, "zl", swap)
    reach = ancestors(lax.dynamic_slice_in_dim(parents, y, 1, 0))
    flat_prior = prior.reshape(-1, DH, DH)
    own_prior = lax.dynamic_index_in_dim(flat_prior, y * SIDE + x, 0, keepdims=False)
    inner = inside(q, k, v, 0, requests)
    got, reach, own_prior, inner = lax.optimization_barrier((got, reach, own_prior, inner))

    pieces = tree(at, got, own_prior, reach)
    from_c = lax.ppermute(pieces[1], "c", swap)
    from_z = lax.ppermute(pieces[2], "zl", swap)
    from_zc = lax.ppermute(pieces[3], quad, crossed)
    before = prefixes(at, got, own_prior)
    from_c, from_z, from_zc, *before = lax.optimization_barrier(
        (from_c, from_z, from_zc, *before)
    )
    mine = jnp.concatenate((pieces[0], from_c, from_z, from_zc))
    heads = exchanged([mine] * SIDE, "x")
    beside = exchanged(before, "x")
    row_of_heads = jnp.concatenate(heads)
    rows = exchanged([row_of_heads] * SIDE, "y")
    w_c = lax.ppermute(weight, "c", swap)
    w_zc = lax.ppermute(w_z, "c", swap)
    states = exchanged(regrouped(at, beside), "y")

    parts = project(at, rows, (weight, w_c, w_z, w_zc))
    total = parts[0].astype(F32)
    shares = exchanged(parts, "zp")
    for got in shares[1:]:
        total = total + got.astype(F32)
    verified = total.astype(BF)

    prefill_out = finish(at, q, inner, states)
    return prefill_out, verified


def solution(mesh):
    torus = Mesh(mesh.devices.reshape(4, 4, 4, 2, 2), (*SEQ, *HEAD))
    return jax.shard_map(
        on_device,
        mesh=torus,
        in_specs=(
            P(None, SEQ, HEAD),
            P(None, SEQ, HEAD),
            P(None, SEQ, HEAD),
            P(None, HEAD, None, None),
            P(None, SEQ, HEAD),
            P(None, SEQ, HEAD),
            P(None, SEQ, HEAD),
            P(),
            P(HEAD, SEQ),
        ),
        out_specs=(P(None, SEQ, HEAD), P(HEAD, SEQ)),
        check_vma=False,
    )
```

```python
import jax
import jax.numpy as jnp
from jax import lax
from jax.experimental import pallas as pl
from jax.experimental.pallas import tpu as pltpu
from jax.sharding import Mesh
from jax.sharding import PartitionSpec as P

DH = 128
NODES = 256
SEQ = ("y", "x")
HEAD = ("zp", "zl", "c")
SIDE = 4
EPS = 1e-05
BF = jnp.bfloat16
F32 = jnp.float32


def mm(a, b, ca, cb):
    return lax.dot_general(a, b, (((ca,), (cb,)), ((), ())), preferred_element_type=F32)


def normed(raw):
    return raw * lax.rsqrt(jnp.mean(raw * raw, axis=-1, keepdims=True) + EPS)


def room(mib):
    return pltpu.CompilerParams(vmem_limit_bytes=mib << 20)


def far(array):
    return pltpu.with_memory_space_constraint(array, pltpu.HBM)


def cost(flops, nbytes):
    return pl.CostEstimate(flops=flops, bytes_accessed=nbytes, transcendentals=0)


def smem():
    return pl.BlockSpec(memory_space=pltpu.SMEM)


def vmem(count):
    return [pl.BlockSpec(memory_space=pltpu.VMEM)] * count


def like(shape, dtype=BF):
    return jax.ShapeDtypeStruct(shape, dtype)


def small(body, outs, scratch=(), flops=0):
    def call(at, *arrays):
        nbytes = sum(a.size * a.dtype.itemsize for a in arrays)
        return pl.pallas_call(
            body,
            in_specs=[smem()] + vmem(len(arrays)),
            out_specs=vmem(len(outs)),
            out_shape=list(outs),
            scratch_shapes=list(scratch),
            cost_estimate=cost(flops, 2 * nbytes),
            compiler_params=room(8),
        )(at, *arrays)

    return call


def states_body(k_ref, v_ref, tq_ref, tk_ref, tv_ref, o_ref, ks, vs, ts, outs, sems, done):
    requests, tokens = k_ref.shape[:2]
    nodes, half = tq_ref.shape[1], tokens // 2
    thin = [
        pltpu.make_async_copy(ref, ts.at[j], sems.at[2, j])
        for j, ref in enumerate((tq_ref, tk_ref, tv_ref))
    ]
    steps = [(r, slice(t * half, (t + 1) * half)) for r in range(requests) for t in range(2)]
    loads = [
        [
            pltpu.make_async_copy(ref.at[r, rows], buf.at[r, rows], sems.at[m, n])
            for m, (ref, buf) in enumerate(((k_ref, ks), (v_ref, vs)))
        ]
        for n, (r, rows) in enumerate(steps)
    ]
    stores = [
        pltpu.make_async_copy(
            outs.at[r * SIDE : (r + 1) * SIDE], o_ref.at[r * SIDE : (r + 1) * SIDE], done.at[r]
        )
        for r in range(requests)
    ]
    for copy in thin + sum(loads, []):
        copy.start()
    for n, (r, rows) in enumerate(steps):
        for copy in loads[n]:
            copy.wait()
        if n == 0:
            for copy in thin:
                copy.wait()
        if n % 2 == 0:
            total = [None] * SIDE
        for pair in range(SIDE // 2):
            cols = slice(2 * pair * DH, 2 * (pair + 1) * DH)
            both = mm(ks[r, rows, cols], vs[r, rows, cols], 0, 0)
            for h in range(2):
                kv = both[h * DH : (h + 1) * DH, h * DH : (h + 1) * DH]
                at = 2 * pair + h
                total[at] = kv if n % 2 == 0 else total[at] + kv
        if n % 2 == 1:
            for h in range(SIDE):
                outs[r * SIDE + h, 0:DH, :] = total[h].astype(BF)
                for j in range(3):
                    rows_at = slice(DH + j * nodes, DH + (j + 1) * nodes)
                    outs[r * SIDE + h, rows_at, :] = ts[j, r, :, h * DH : (h + 1) * DH]
            stores[r].start()
    for copy in stores:
        copy.wait()


def block_states(k, v, tq, tk, tv):
    requests, tokens, width = k.shape
    nodes = tq.shape[1]
    rows = DH + 3 * nodes
    return pl.pallas_call(
        states_body,
        in_specs=[pl.BlockSpec(memory_space=pltpu.HBM)] * 5,
        out_specs=pl.BlockSpec(memory_space=pltpu.HBM),
        out_shape=pltpu.HBM((requests * SIDE, rows, DH), BF),
        scratch_shapes=[
            pltpu.VMEM(k.shape, BF),
            pltpu.VMEM(v.shape, BF),
            pltpu.VMEM((3, *tq.shape), BF),
            pltpu.VMEM((requests * SIDE, rows, DH), BF),
            pltpu.SemaphoreType.DMA((3, 2 * requests)),
            pltpu.SemaphoreType.DMA((requests,)),
        ],
        cost_estimate=cost(2 * requests * tokens * width * DH, 4 * requests * tokens * width),
        compiler_params=room(16),
        name="block_states",
    )(far(k), far(v), far(tq), far(tk), far(tv))


def reach_body(parents_ref, o_ref):
    row = lax.broadcasted_iota(jnp.int32, (NODES, NODES), 0)
    col = lax.broadcasted_iota(jnp.int32, (NODES, NODES), 1)
    links = (parents_ref[...] == row) & (col >= 1)
    reach = jnp.where(links | (row == col), 1.0, 0.0).astype(BF)
    for _ in range((NODES - 1).bit_length()):
        reach = jnp.minimum(mm(reach, reach, 1, 0), 1.0).astype(BF)
    o_ref[...] = reach.astype(F32).T


def ancestors(own_parents):
    return pl.pallas_call(
        reach_body,
        out_shape=like((NODES, NODES), F32),
        cost_estimate=cost(16 * NODES**3, 4 * NODES * NODES),
        compiler_params=room(4),
        name="ancestors",
    )(own_parents)


def tree_body(at_ref, got_ref, prior_ref, reach_ref, *refs):
    outs, hold = refs[:-1], refs[-1]
    peers = got_ref.shape[0]
    nodes = NODES // peers
    total = prior_ref[...]
    for s in range(peers):
        total = total + got_ref[s, 0:DH, :].astype(F32)

    def part(j):
        start = DH + j * nodes
        return got_ref[:, start : start + nodes, :].reshape(NODES, DH)

    q, k, v = part(0), part(1), part(2)
    weights = jnp.where(reach_ref[...] > 0, mm(q, k, 1, 1), 0.0).astype(BF)
    raw = mm(q, total.astype(BF), 1, 0) + mm(weights, v, 1, 0)
    hold[...] = normed(raw).astype(BF).reshape(hold.shape)
    for j, out in enumerate(outs):
        out[...] = hold[at_ref[3] ^ j]


def tree(at, got, prior, reach):
    nodes = NODES // SIDE
    scratch = [pltpu.VMEM((SIDE, nodes, DH), BF)]
    call = small(tree_body, [like((nodes, DH))] * SIDE, scratch, 6 * NODES * NODES * DH)
    return call(at, got, prior, reach)


def prefix_body(at_ref, got_ref, prior_ref, *refs):
    outs, hold = refs[:-1], refs[-1]
    running = prior_ref[...]
    for y in range(SIDE):
        for x in range(SIDE):
            hold[y, x] = running.astype(BF)
            running = running + got_ref[y * SIDE + x, 0:DH, :].astype(F32)
    for s, out in enumerate(outs):
        for y in range(SIDE):
            out[y] = hold[y, at_ref[0] ^ s]


def prefixes(at, got, prior):
    scratch = [pltpu.VMEM((SIDE, SIDE, DH, DH), BF)]
    outs = [like((SIDE, DH, DH))] * SIDE
    return small(prefix_body, outs, scratch)(at, got, prior)


def regroup_body(at_ref, *refs):
    got, outs = refs[:SIDE], refs[SIDE:]
    for s, out in enumerate(outs):
        for t in range(SIDE):
            out[at_ref[0] ^ t] = got[t][at_ref[1] ^ s]


def regrouped(at, got):
    return small(regroup_body, [like(got[0].shape)] * SIDE)(at, *got)


def inner_body(q_ref, k_ref, v_ref, o_ref):
    tokens, width = q_ref.shape[1:]
    half = tokens // 2
    for h in range(width // DH):
        cols = slice(h * DH, (h + 1) * DH)
        for part in range(2):
            rows = slice(part * half, (part + 1) * half)
            upto = (part + 1) * half
            scores = mm(q_ref[0, rows, cols], k_ref[0, 0:upto, cols], 1, 1)
            at = part * half + lax.broadcasted_iota(jnp.int32, scores.shape, 0)
            other = lax.broadcasted_iota(jnp.int32, scores.shape, 1)
            weights = jnp.where(at >= other, scores, 0.0).astype(BF)
            o_ref[0, rows, cols] = mm(weights, v_ref[0, 0:upto, cols], 1, 0).astype(BF)


def inside(q, k, v, first, count, onto=None):
    _, tokens, width = q.shape
    big = pl.BlockSpec((1, tokens, width), lambda r: (r + first, 0, 0))
    more = [] if onto is None else [onto]
    body = inner_body if onto is None else lambda q, k, v, _, o: inner_body(q, k, v, o)
    return pl.pallas_call(
        body,
        grid=(count,),
        in_specs=[big, big, big] + [pl.BlockSpec(memory_space=pltpu.HBM)] * len(more),
        out_specs=big,
        out_shape=pltpu.HBM(q.shape, BF),
        input_output_aliases={3: 0} if more else {},
        cost_estimate=cost(3 * count * tokens * tokens * width, 8 * count * tokens * width),
        compiler_params=room(24),
        name="inside",
    )(far(q), far(k), far(v), *more)


def finish_body(at_ref, q_ref, inner_ref, *refs):
    states, (o_ref, hold, outs, sems) = refs[:SIDE], refs[SIDE:]
    requests, _, _ = q_ref.shape
    for s in range(SIDE):
        hold[at_ref[1] ^ s] = states[s][...]
    stores = [pltpu.make_async_copy(outs.at[r], o_ref.at[r], sems.at[r]) for r in range(requests)]
    for r in range(requests):
        for h in range(SIDE):
            cols = slice(h * DH, (h + 1) * DH)
            raw = mm(q_ref[r, :, cols], hold[r, h], 1, 0) + inner_ref[r, :, cols].astype(F32)
            outs[r, :, cols] = normed(raw).astype(BF)
        stores[r].start()
    for copy in stores:
        copy.wait()


def finish(at, q, inner, states):
    requests, tokens, width = q.shape
    return pl.pallas_call(
        finish_body,
        in_specs=[smem()] + vmem(2 + SIDE),
        out_specs=pl.BlockSpec(memory_space=pltpu.HBM),
        out_shape=like(q.shape),
        scratch_shapes=[
            pltpu.VMEM((SIDE, requests, DH, DH), BF),
            pltpu.VMEM(q.shape, BF),
            pltpu.SemaphoreType.DMA((requests,)),
        ],
        cost_estimate=cost(2 * requests * tokens * width * DH, 6 * requests * tokens * width),
        compiler_params=room(16),
        name="finish",
    )(at, q, inner, *states)


def project_body(at_ref, *refs):
    rows, weights, outs = refs[:SIDE], refs[SIDE : 2 * SIDE], refs[2 * SIDE : 3 * SIDE]
    hold = refs[-1]
    nodes = outs[0].shape[0]
    total = None
    for j in range(SIDE):
        parts = []
        for t in range(SIDE):
            heads = [
                rows[t][pl.ds((at_ref[0] ^ h) * NODES + j * nodes, nodes), :]
                for h in range(SIDE)
            ]
            parts.append(jnp.concatenate(heads, axis=1))
        lhs = jnp.concatenate(parts, axis=0)
        part = mm(lhs, weights[j][...], 1, 0)
        total = part if total is None else total + part
    hold[...] = total.astype(BF).reshape(hold.shape)
    for s, out in enumerate(outs):
        out[...] = hold[at_ref[1] ^ at_ref[2] ^ s]


def project(at, rows, weights):
    nodes = NODES // SIDE
    deep, wide = weights[0].shape
    return pl.pallas_call(
        project_body,
        in_specs=[smem()] + vmem(2 * SIDE),
        out_specs=vmem(SIDE),
        scratch_shapes=[
            pltpu.VMEM((SIDE, nodes, wide), BF),
        ],
        out_shape=[like((nodes, wide))] * SIDE,
        cost_estimate=cost(2 * SIDE * SIDE * NODES * DH * wide, 8 * deep * wide),
        compiler_params=room(8),
        name="project",
    )(at, *rows, *weights)


def exchanged(arrays, axis):
    got = [arrays[0]]
    for s in range(1, SIDE):
        got.append(lax.ppermute(arrays[s], axis, [(i, i ^ s) for i in range(SIDE)]))
    return got


def on_device(q, k, v, prior, tq, tk, tv, parents, weight):
    requests, _, _ = q.shape
    x, y, zp = (lax.axis_index(name) for name in ("x", "y", "zp"))
    group = lax.axis_index("zl") * 2 + lax.axis_index("c")
    at = jnp.stack([x, y, zp, group]).astype(jnp.int32)

    swap = [(0, 1), (1, 0)]
    quad = ("zl", "c")
    crossed = [(g, g ^ 3) for g in range(SIDE)]

    sent = block_states(k, v, tq, tk, tv)
    got = lax.all_to_all(sent, SEQ, 0, 0, tiled=True)
    weight, _ = lax.optimization_barrier((weight, sent))
    w_z = lax.ppermute(weight, "zl", swap)
    reach = ancestors(lax.dynamic_slice_in_dim(parents, y, 1, 0))
    flat_prior = prior.reshape(-1, DH, DH)
    own_prior = lax.dynamic_index_in_dim(flat_prior, y * SIDE + x, 0, keepdims=False)
    inner = inside(q, k, v, 0, requests)
    got, reach, own_prior, inner = lax.optimization_barrier((got, reach, own_prior, inner))

    pieces = tree(at, got, own_prior, reach)
    from_c = lax.ppermute(pieces[1], "c", swap)
    from_z = lax.ppermute(pieces[2], "zl", swap)
    from_zc = lax.ppermute(pieces[3], quad, crossed)
    before = prefixes(at, got, own_prior)
    from_c, from_z, from_zc, *before = lax.optimization_barrier(
        (from_c, from_z, from_zc, *before)
    )
    mine = jnp.concatenate((pieces[0], from_c, from_z, from_zc))
    heads = exchanged([mine] * SIDE, "x")
    beside = exchanged(before, "x")
    row_of_heads = jnp.concatenate(heads)
    rows = exchanged([row_of_heads] * SIDE, "y")
    w_c = lax.ppermute(weight, "c", swap)
    w_zc = lax.ppermute(w_z, "c", swap)
    states = exchanged(regrouped(at, beside), "y")

    parts = project(at, rows, (weight, w_c, w_z, w_zc))
    total = parts[0].astype(F32)
    shares = exchanged(parts, "zp")
    for got in shares[1:]:
        total = total + got.astype(F32)
    verified = total.astype(BF)

    prefill_out = finish(at, q, inner, states)
    return prefill_out, verified


def solution(mesh):
    torus = Mesh(mesh.devices.reshape(4, 4, 4, 2, 2), (*SEQ, *HEAD))
    return jax.shard_map(
        on_device,
        mesh=torus,
        in_specs=(
            P(None, SEQ, HEAD),
            P(None, SEQ, HEAD),
            P(None, SEQ, HEAD),
            P(None, HEAD, None, None),
            P(None, SEQ, HEAD),
            P(None, SEQ, HEAD),
            P(None, SEQ, HEAD),
            P(),
            P(HEAD, SEQ),
        ),
        out_specs=(P(None, SEQ, HEAD), P(HEAD, SEQ)),
        check_vma=False,
    )
```
